256 devices in a mesh: ctx: 64 (over y, x, z_lo, core), grp: 4 (over z_hi).
Axes of the slice: x: 4, y: 4, z: 8 (z_hi: 4, z_lo: 2; z = z_hi * 2 + z_lo), core: 2. Of those that a mesh axis runs over, the one named last changes fastest.
Arguments:
- saved_input: bfloat16 [4, 2048, 8192], P('grp', None, 'ctx'), may hold values from -6 to 6
- out_grad: bfloat16 [4, 2048, 8192], P('grp', None, 'ctx'), may hold values from -0.0625 to 0.0625
- filters: float32 [4, 2048, 8192], P('grp', 'ctx'), may hold values from -6 to 6
- adapter_down: bfloat16 [16, 4, 2048], P(None, 'grp'), may hold values from -0.0625 to 0.0625
- adapter_up: bfloat16 [16, 4, 2048], P(None, 'grp'), may hold values from -0.25 to 0.25
Outputs:
- grad_input: bfloat16 [4, 2048, 8192], P('grp', None, 'ctx')
- grad_filter: float32 [4, 2048, 8192], P('grp', 'ctx')
- grad_down: float32 [16, 4, 2048], P(None, 'grp')
- grad_up: float32 [16, 4, 2048], P(None, 'grp')
The draws below stay inside these ranges and needn't reach their ends.
All inputs are finite; a program needn't handle non-finite values.
Results may differ from the reference program's by a relative error of at most 0.0075.
Values may be sent and summed in bfloat16 or wider, within the bound.
A program may use at most 64 MiB of HBM per device.

```python
import jax
import jax.numpy as jnp
from jax import lax

D = 8192
RANK = 16
TOKENS = 8192
GROUPS = 4
GW = 2048


def shard_levels(own_key, dims, cuts, smallest, top_value):
    gain, own = 1.0, jax.random.fold_in(own_key, 6)
    for dim, blocks in cuts:
        heights = jnp.exp(jax.random.uniform(jax.random.fold_in(own, dim), (blocks,), jnp.float32, smallest / len(cuts), top_value / len(cuts)))
        gain = gain * jnp.repeat(heights, dims[dim] // blocks).reshape([-1 if axis == dim else 1 for axis in range(len(dims))])
    return gain


def centred(own_key, extent, spread, most, shards=(), kind=jnp.bfloat16):
    entries = spread * jax.random.normal(own_key, extent, jnp.float32)
    if shards:
        entries = entries * shard_levels(own_key, extent, shards, -0.22, 0.18)
    return jnp.clip(entries, -most, most).astype(kind)


def setup_inputs(seed: int = 0) -> dict:
    arg_keys = jax.random.split(jax.random.key(seed), 6)
    return {
        "saved_input": centred(arg_keys[0], (GROUPS, GW, TOKENS), 1.0, 6.0, ((0, 4), (2, 64))),
        "out_grad": centred(arg_keys[1], (GROUPS, GW, TOKENS), TOKENS ** -0.5, 0.0625, ((0, 4), (2, 64))),
        "filters": centred(arg_keys[2], (GROUPS, GW, TOKENS), 1.0, 6.0, ((0, 4), (1, 64)), jnp.float32),
        "adapter_down": centred(arg_keys[3], (RANK, GROUPS, GW), D ** -0.5, 0.0625, ((1, 4),)),
        "adapter_up": centred(arg_keys[4], (RANK, GROUPS, GW), (D // 16) ** -0.5, 0.25, ((1, 4),)),
    }


HIGH = lax.Precision.HIGHEST


def convolve_group(operands):
    adapted, gradient, kernel = operands
    points = 2 * TOKENS
    act_spec = jnp.fft.rfft(adapted.astype(jnp.float32), n=points, axis=-1)
    grad_spec = jnp.fft.rfft(gradient.astype(jnp.float32), n=points, axis=-1)
    kern_spec = jnp.fft.rfft(kernel, n=points, axis=-1)
    grad_u = jnp.fft.irfft(grad_spec * jnp.conj(kern_spec), n=points, axis=-1)[:, :TOKENS]
    grad_filt = jnp.fft.irfft(grad_spec * jnp.conj(act_spec), n=points, axis=-1)[:, :TOKENS]
    return grad_u.astype(jnp.bfloat16), grad_filt


def reference(saved_input, out_grad, filters, adapter_down, adapter_up):
    inputs = saved_input.reshape(D, TOKENS).astype(jnp.float32)
    down_map = adapter_down.reshape(RANK, D).astype(jnp.float32)
    up_map = adapter_up.reshape(RANK, D).astype(jnp.float32)
    rank_acts = jnp.einsum("rc,ct->rt", down_map, inputs, precision=HIGH)
    adapted = (inputs + jnp.einsum("rc,rt->ct", up_map, rank_acts, precision=HIGH)).astype(jnp.bfloat16)
    grad_u, grad_filter = lax.map(convolve_group, (adapted.reshape(GROUPS, GW, TOKENS), out_grad, filters))
    du_float = grad_u.reshape(D, TOKENS).astype(jnp.float32)
    rank_grad = jnp.einsum("rc,ct->rt", up_map, du_float, precision=HIGH)
    grad_input = (du_float + jnp.einsum("rc,rt->ct", down_map, rank_grad, precision=HIGH)).astype(jnp.bfloat16)
    factor = float(TOKENS) ** -0.5
    grad_down = factor * jnp.einsum("rt,ct->rc", rank_grad, inputs, precision=HIGH)
    grad_up = factor * jnp.einsum("rt,ct->rc", rank_acts, du_float, precision=HIGH)
    return (grad_input.reshape(GROUPS, GW, TOKENS), grad_filter.reshape(GROUPS, GW, TOKENS),
            grad_down.reshape(RANK, GROUPS, GW), grad_up.reshape(RANK, GROUPS, GW))
```

```python
import math

import jax
import jax.numpy as jnp
from jax import lax
from jax.sharding import PartitionSpec as P

HIGH = lax.Precision.HIGHEST


def split_radix(points):
    radix_low = 1
    while (
        points % (radix_low * 2) == 0
        and radix_low * 2 * (radix_low * 2) <= points
        and (points // (radix_low * 2) % 2 == 0)
    ):
        radix_low = radix_low * 2
    return (radix_low, points // radix_low)


def angle_table(height, across, period):
    index_down = lax.broadcasted_iota(jnp.int32, (height, across), 0)
    index_across = lax.broadcasted_iota(jnp.int32, (height, across), 1)
    phase = (index_down * index_across % period).astype(jnp.float32) * (2.0 * math.pi / period)
    return (jnp.cos(phase), jnp.sin(phase))


def make_tables(points):
    radix_low, radix_high = split_radix(points)
    cos_one, sin_one = angle_table(radix_high, radix_high // 2, radix_high)
    first = jnp.concatenate([cos_one, -sin_one], axis=0)
    first_high = first.astype(jnp.bfloat16)
    first_low = (first - first_high.astype(jnp.float32)).astype(jnp.bfloat16)
    twist = angle_table(radix_high, radix_low, points)
    cos_two, sin_two = angle_table(radix_low, radix_low, radix_low)
    second_fwd = jnp.concatenate(
        [jnp.concatenate([cos_two, sin_two], axis=1), jnp.concatenate([-sin_two, cos_two], axis=1)],
        axis=0,
    )
    second_inv = jnp.concatenate(
        [jnp.concatenate([cos_two, -sin_two], axis=1), jnp.concatenate([sin_two, cos_two], axis=1)],
        axis=0,
    )
    last_inv = jnp.concatenate([cos_one, -sin_one], axis=0)
    return (
        radix_low,
        radix_high,
        first,
        first_high,
        first_low,
        twist,
        second_fwd,
        second_inv,
        last_inv,
    )


def forward_dft(signal, tables):
    radix_low, radix_high, first, first_high, first_low, twist, second_fwd, second_inv, last_inv = (
        tables
    )
    channels = signal.shape[0]
    blocks = signal.reshape(channels, radix_high // 2, radix_low)
    if signal.dtype == jnp.bfloat16:
        section_one = jnp.einsum(
            "kn,cnp->ckp", first_high, blocks, preferred_element_type=jnp.float32
        )
        section_one = section_one + jnp.einsum(
            "kn,cnp->ckp", first_low, blocks, preferred_element_type=jnp.float32
        )
    else:
        section_one = jnp.einsum("kn,cnp->ckp", first, blocks, precision=HIGH)
    real_one = section_one[:, :radix_high]
    imag_one = section_one[:, radix_high:]
    cos_twist, sin_twist = twist
    real_two = real_one * cos_twist + imag_one * sin_twist
    imag_two = imag_one * cos_twist - real_one * sin_twist
    joined = jnp.concatenate([real_two, imag_two], axis=2)
    spectrum = jnp.einsum("jq,ckq->cjk", second_fwd, joined, precision=HIGH)
    return (spectrum[:, :radix_low], spectrum[:, radix_low:])


def inverse_dft(spectrum, tables):
    radix_low, radix_high, first, first_high, first_low, twist, second_fwd, second_inv, last_inv = (
        tables
    )
    spec_real, spec_imag = spectrum
    channels = spec_real.shape[0]
    joined = jnp.concatenate([spec_real, spec_imag], axis=1)
    section_one = jnp.einsum("pq,cqk->cpk", second_inv, joined, precision=HIGH)
    real_one = section_one[:, :radix_low]
    imag_one = section_one[:, radix_low:]
    cos_twist = twist[0].T
    sin_twist = twist[1].T
    real_two = real_one * cos_twist - imag_one * sin_twist
    imag_two = real_one * sin_twist + imag_one * cos_twist
    stacked = jnp.concatenate([real_two, imag_two], axis=2)
    signal = jnp.einsum("kn,cpk->cnp", last_inv, stacked, precision=HIGH)
    return signal.reshape(channels, -1) / float(radix_low * radix_high)


def conj_product(spec_left, spec_right):
    left_real, left_imag = spec_left
    right_real, right_imag = spec_right
    return (
        left_real * right_real + left_imag * right_imag,
        left_imag * right_real - left_real * right_imag,
    )


def body(saved_input, out_grad, filters, adapter_down, adapter_up):
    tok_input = saved_input[0]
    tok_grad = out_grad[0]
    down_rows = adapter_down[:, 0, :]
    up_float = adapter_up[:, 0, :].astype(jnp.float32)
    rank_part = jnp.dot(down_rows, tok_input, preferred_element_type=jnp.float32)
    rank_acts = lax.psum(rank_part, "grp")
    tok_act = (
        tok_input.astype(jnp.float32) + jnp.einsum("rc,rt->ct", up_float, rank_acts, precision=HIGH)
    ).astype(jnp.bfloat16)
    chan_act, chan_grad = (
        lax.all_to_all(tok_act, "ctx", split_axis=0, concat_axis=1, tiled=True),
        lax.all_to_all(tok_grad, "ctx", split_axis=0, concat_axis=1, tiled=True),
    )
    length = chan_act.shape[1]
    tables = make_tables(2 * length)
    act_spec = forward_dft(chan_act, tables)
    grad_spec = forward_dft(chan_grad, tables)
    kern_spec = forward_dft(filters[0], tables)
    chan_du = inverse_dft(conj_product(grad_spec, kern_spec), tables).astype(jnp.bfloat16)
    filt_grad = inverse_dft(conj_product(grad_spec, act_spec), tables)
    tok_du = lax.all_to_all(chan_du, "ctx", split_axis=1, concat_axis=0, tiled=True)
    du_float = tok_du.astype(jnp.float32)
    rank_grad = lax.psum(jnp.einsum("rc,ct->rt", up_float, du_float, precision=HIGH), "grp")
    grad_input = (
        du_float + jnp.einsum("rc,rt->ct", down_rows.astype(jnp.float32), rank_grad, precision=HIGH)
    ).astype(jnp.bfloat16)
    down_part = jnp.einsum("rt,ct->rc", rank_grad, tok_input.astype(jnp.float32), precision=HIGH)
    up_part = jnp.einsum("rt,ct->rc", rank_acts, du_float, precision=HIGH)
    parts = jnp.concatenate([down_part, up_part], axis=0)
    rows, width = parts.shape
    tiles = parts.reshape(rows // 8, 8, width // 128, 128).transpose(0, 2, 1, 3).reshape(-1, 8, 128)
    shares = lax.all_to_all(tiles, "ctx", split_axis=0, concat_axis=0, tiled=True)
    own = jnp.sum(shares, axis=0)
    copies = jnp.broadcast_to(own[None], shares.shape)
    every = lax.all_to_all(copies, "ctx", split_axis=0, concat_axis=0, tiled=True)
    sums = every.reshape(rows // 8, width // 128, 8, 128).transpose(0, 2, 1, 3).reshape(rows, width)
    down_sum, up_sum = sums[: rows // 2], sums[rows // 2 :]
    factor = float(length) ** (-0.5)
    return (
        grad_input[None],
        filt_grad[None],
        (factor * down_sum)[:, None, :],
        (factor * up_sum)[:, None, :],
    )


def solution(mesh):
    placed = (
        P("grp", None, "ctx"),
        P("grp", None, "ctx"),
        P("grp", "ctx", None),
        P(None, "grp", None),
        P(None, "grp", None),
    )
    return jax.shard_map(
        body,
        mesh=mesh,
        in_specs=placed,
        out_specs=(
            P("grp", None, "ctx"),
            P("grp", "ctx", None),
            P(None, "grp", None),
            P(None, "grp", None),
        ),
        check_vma=False,
    )
```

```python
import functools
import math

import jax
import jax.numpy as jnp
import numpy as np
from jax import lax
from jax.experimental import pallas as pl
from jax.experimental.pallas import tpu as pltpu
from jax.sharding import PartitionSpec as P

MESH = pl.DeviceIdType.MESH
F32 = jnp.float32
BF16 = jnp.bfloat16
LANES = 128
CHANS = 32
STEP = 8
GRID = {64: (4, 4, 2, 2), 8: (2, 2, 2, 1)}
SCRAMBLE = 29


def halves(table):
    high = table.astype(BF16)
    low = (table - high.astype(np.float64)).astype(BF16)
    return high, low


def make_tables(rows):
    points = 2 * rows * LANES
    n = np.arange(rows)
    p = np.arange(LANES)
    theta = np.outer(n + 0.5, n) * (2.0 * math.pi / (2 * rows))
    phi = np.outer(p, p) * (2.0 * math.pi / LANES)
    turn = np.outer(n + 0.5, p) * (2.0 * math.pi / points)
    high, low = halves(np.concatenate([np.cos(theta), -np.sin(theta)], axis=0))
    first_two = np.concatenate([high, low], axis=1)
    first_three = np.concatenate([high, high, low], axis=1)
    cos, sin = np.cos(phi), np.sin(phi)
    high, low = halves(np.block([[cos, -sin], [sin, cos]]))
    second = np.concatenate([high, high, low], axis=0)
    high, low = halves(np.block([[cos, sin], [-sin, cos]]))
    third = np.concatenate([high, high, low], axis=0)
    high, low = halves(np.concatenate([np.cos(theta).T, -np.sin(theta).T], axis=1) * (2.0 / points))
    last = np.concatenate([high, high, low], axis=1)
    twist = np.stack([np.cos(turn), np.sin(turn)]).astype(np.float32)
    return first_two, first_three, twist, second, third, last


def split(value):
    high = value.astype(BF16)
    return high, (value - high.astype(F32)).astype(BF16)


def dot(left, right, dims=((1,), (0,))):
    return lax.dot_general(left, right, (dims, ((), ())), preferred_element_type=F32)


def gather_rows(ref, first, rows):
    blocks = [ref[pl.ds(first + j, rows, stride=CHANS), :] for j in range(STEP)]
    return jnp.concatenate(blocks, axis=1)


def forward(data, first, twist, second, exact):
    rows = data.shape[0]
    if exact:
        narrow = data.astype(BF16)
        stacked = jnp.concatenate([narrow, narrow], axis=0)
    else:
        high, low = split(data)
        stacked = jnp.concatenate([high, low, high], axis=0)
    part = dot(first[...], stacked)
    cos, sin = twist[0], twist[1]
    joined = []
    for j in range(STEP):
        lanes = slice(j * LANES, (j + 1) * LANES)
        real, imag = part[:rows, lanes], part[rows:, lanes]
        joined.append(jnp.concatenate([real * cos + imag * sin, imag * cos - real * sin], axis=1))
    high, low = split(jnp.concatenate(joined, axis=0))
    return dot(jnp.concatenate([high, low, high], axis=1), second[...])


def inverse(spectrum, twist, third, last):
    rows = twist.shape[1]
    high, low = split(spectrum)
    part = dot(jnp.concatenate([high, low, high], axis=1), third[...])
    cos, sin = twist[0], twist[1]
    reals, imags = [], []
    for j in range(STEP):
        real = part[j * rows : (j + 1) * rows, :LANES]
        imag = part[j * rows : (j + 1) * rows, LANES:]
        reals.append(real * cos - imag * sin)
        imags.append(real * sin + imag * cos)
    joined = jnp.concatenate([jnp.concatenate(reals, axis=1), jnp.concatenate(imags, axis=1)], axis=0)
    high, low = split(joined)
    return dot(last[...], jnp.concatenate([high, low, high], axis=0))


def conj_product(left, right):
    lr, li = left[:, :LANES], left[:, LANES:]
    rr, ri = right[:, :LANES], right[:, LANES:]
    return jnp.concatenate([lr * rr + li * ri, li * rr - lr * ri], axis=1)


def kernel(
    count, groups, factor,
    x_hbm, dy_hbm, h_hbm, a_ref, b_ref, first_two, first_three, twist, second, third, last,
    gi_hbm, gf_hbm, gd_ref, gu_ref,
    x_buf, h_buf, u_buf, du_buf, gi_buf, dy_got, u_got, du_got, wide, work, gf_buf,
    spec_h, spec_dy, z_mine, z_got, r_mine, r_got, parts, part_got, total, total_got,
    load_sem, send_sem, recv_sem,
):
    me = lax.axis_index("ctx")
    grp = lax.axis_index("grp")
    sizes = GRID[count]
    coords, rest = [], me
    for size in reversed(sizes):
        coords.append(rest % size)
        rest = rest // size
    width = count * CHANS

    def peer_of(d):
        rest, stride, peer = (d * SCRAMBLE) % count, 1, 0
        for size, own in zip(reversed(sizes), coords):
            peer = peer + ((own + rest % size) % size) * stride
            rest = rest // size
            stride = stride * size
        return peer

    def each_peer(action):
        def run(d, carry):
            action(peer_of(d))
            return carry

        lax.fori_loop(1, count, run, 0)

    def each_group(action):
        for e in range(1, groups):
            action(lax.rem(grp + e, groups))

    def send(src, dst, slot, target):
        pltpu.make_async_remote_copy(
            src_ref=src, dst_ref=dst, send_sem=send_sem.at[slot], recv_sem=recv_sem.at[slot],
            device_id=target, device_id_type=MESH,
        ).start()

    def wait_for(sems, slot, ref):
        pltpu.make_async_copy(ref, ref, sems.at[slot]).wait()

    barrier = pltpu.get_barrier_semaphore()

    def greet(target):
        pl.semaphore_signal(barrier, inc=1, device_id=target, device_id_type=MESH)

    each_peer(lambda p: greet({"ctx": p}))
    each_group(lambda g: greet({"grp": g}))

    x_load = pltpu.make_async_copy(x_hbm, x_buf, load_sem.at[0])
    x_load.start()

    def load_h(n, carry):
        lanes = pl.ds(pl.multiple_of(n * LANES, LANES), LANES)
        rows = pl.ds(pl.multiple_of(n * CHANS, CHANS), CHANS)
        pltpu.make_async_copy(h_hbm.at[:, lanes], h_buf.at[rows], load_sem.at[1]).start()
        return carry

    lax.fori_loop(0, count, load_h, 0)
    own_rows = pl.ds(pl.multiple_of(me * CHANS, CHANS), CHANS)
    own_dy = pltpu.make_async_copy(dy_hbm.at[own_rows], dy_got.at[me], load_sem.at[2])
    own_dy.start()
    x_load.wait()
    z_part = dot(a_ref[...], x_buf[...])
    z_mine[...] = z_part
    pl.semaphore_wait(barrier, count - 1 + groups - 1)

    each_group(lambda g: send(z_mine, z_got.at[grp], 0, {"grp": g}))

    def send_dy(p):
        rows = pl.ds(pl.multiple_of(p * CHANS, CHANS), CHANS)
        send(dy_hbm.at[rows], dy_got.at[me], 1, {"ctx": p})

    each_peer(send_dy)

    pltpu.make_async_copy(h_buf, h_buf, load_sem.at[1]).wait()

    def spectrum_h(i, carry):
        data = gather_rows(h_buf, i * STEP, count)
        spec_h[pl.ds(pl.multiple_of(i * STEP * count, STEP * count), STEP * count), :] = forward(
            data, first_three, twist, second, False
        )
        return carry

    lax.fori_loop(0, CHANS // STEP, spectrum_h, 0)

    def shared_sum(mine, got):
        got[grp] = mine[...]
        acc = got[0]
        for g in range(1, groups):
            acc = acc + got[g]
        return acc

    def low_rank(base, maps, value, out):
        high, low = split(value)
        pair = jnp.concatenate([high, low], axis=0)
        chunk = 256
        for start in range(0, width, chunk):
            left = maps[:, start : start + chunk]
            left = jnp.concatenate([left, left], axis=0)
            low_part = dot(left, pair, ((0,), (0,)))
            out[start : start + chunk, :] = (base(start, chunk).astype(F32) + low_part).astype(BF16)

    wait_for(recv_sem, 0, z_got.at[pl.ds(0, groups - 1)])
    z = shared_sum(z_mine, z_got)
    low_rank(lambda s, n: x_buf[s : s + n, :], b_ref, z, u_buf)
    u_got[me] = u_buf[own_rows, :]

    def send_u(p):
        rows = pl.ds(pl.multiple_of(p * CHANS, CHANS), CHANS)
        send(u_buf.at[rows], u_got.at[me], 2, {"ctx": p})

    each_peer(send_u)

    others = pl.ds(0, count - 1)
    own_dy.wait()
    wait_for(recv_sem, 1, dy_got.at[others])

    def widen(got):
        def run(n, carry):
            rows = pl.ds(pl.multiple_of(n * CHANS, CHANS), CHANS)
            wide[rows, :] = got[n].astype(F32)
            return carry

        lax.fori_loop(0, count, run, 0, unroll=8)

    def scatter_rows(ref, first, value):
        for j in range(STEP):
            ref[pl.ds(first + j, count, stride=CHANS), :] = value[:, j * LANES : (j + 1) * LANES]

    widen(dy_got)

    def conv_grad(i, carry):
        rows = pl.ds(pl.multiple_of(i * STEP * count, STEP * count), STEP * count)
        spec = forward(gather_rows(wide, i * STEP, count), first_two, twist, second, True)
        spec_dy[rows, :] = spec
        scatter_rows(work, i * STEP, inverse(conj_product(spec, spec_h[rows, :]), twist, third, last))
        return carry

    lax.fori_loop(0, CHANS // STEP, conv_grad, 0)
    def narrow(n, carry):
        rows = pl.ds(pl.multiple_of(n * CHANS, CHANS), CHANS)
        du_buf[rows, :] = work[rows, :].astype(BF16)
        return carry

    lax.fori_loop(0, count, narrow, 0, unroll=8)
    du_got[own_rows, :] = du_buf[own_rows, :]

    def send_du(p):
        rows = pl.ds(pl.multiple_of(p * CHANS, CHANS), CHANS)
        send(du_buf.at[rows], du_got.at[own_rows], 3, {"ctx": p})

    each_peer(send_du)

    wait_for(recv_sem, 2, u_got.at[others])
    widen(u_got)

    def filter_grad(i, carry):
        rows = pl.ds(pl.multiple_of(i * STEP * count, STEP * count), STEP * count)
        spec = forward(gather_rows(wide, i * STEP, count), first_two, twist, second, True)
        scatter_rows(gf_buf, i * STEP, inverse(conj_product(spec_dy[rows, :], spec), twist, third, last))
        return carry

    lax.fori_loop(0, CHANS // STEP, filter_grad, 0)

    def store_gf(n, carry):
        lanes = pl.ds(pl.multiple_of(n * LANES, LANES), LANES)
        rows = pl.ds(pl.multiple_of(n * CHANS, CHANS), CHANS)
        pltpu.make_async_copy(gf_buf.at[rows], gf_hbm.at[:, lanes], load_sem.at[3]).start()
        return carry

    lax.fori_loop(0, count, store_gf, 0)

    wait_for(recv_sem, 3, du_got.at[pl.ds(0, width - CHANS)])
    r_mine[...] = dot(b_ref[...], du_got[...])
    each_group(lambda g: send(r_mine, r_got.at[grp], 4, {"grp": g}))

    ranks = z_mine.shape[0]
    blocks = width // LANES

    def outer(value, tokens, offset):
        high, low = split(value)
        both = dot(jnp.concatenate([high, low], axis=0), tokens, ((1,), (1,)))
        out = (both[:ranks] + both[ranks:]) * factor
        for r in range(ranks // 8):
            for k in range(blocks):
                parts[offset + r * blocks + k] = out[r * 8 : r * 8 + 8, k * LANES : (k + 1) * LANES]

    outer(z, du_got[...], count // 2)
    wait_for(recv_sem, 4, r_got.at[pl.ds(0, groups - 1)])
    rank_grad = shared_sum(r_mine, r_got)
    outer(rank_grad, x_buf[...], 0)
    each_peer(lambda p: send(parts.at[p], part_got.at[me], 5, {"ctx": p}))
    part_got[me] = parts[me]
    low_rank(lambda s, n: du_got[s : s + n, :], a_ref, rank_grad, gi_buf)
    gi_store = pltpu.make_async_copy(gi_buf, gi_hbm, load_sem.at[4])
    gi_store.start()

    wait_for(recv_sem, 5, part_got.at[others])
    acc = jnp.sum(part_got[...], axis=0)
    total[...] = acc
    total_got[me] = acc
    each_peer(lambda p: send(total, total_got.at[me], 6, {"ctx": p}))
    wait_for(recv_sem, 6, total_got.at[others])
    for r in range(ranks // 8):
        for k in range(blocks):
            rows, lanes = slice(r * 8, r * 8 + 8), slice(k * LANES, (k + 1) * LANES)
            gd_ref[rows, lanes] = total_got[r * blocks + k]
            gu_ref[rows, lanes] = total_got[count // 2 + r * blocks + k]

    gi_store.wait()
    pltpu.make_async_copy(gf_buf, gf_buf, load_sem.at[3]).wait()
    wait_for(send_sem, 0, z_got.at[pl.ds(0, groups - 1)])
    wait_for(send_sem, 1, dy_got.at[others])
    wait_for(send_sem, 2, u_got.at[others])
    wait_for(send_sem, 3, du_got.at[pl.ds(0, width - CHANS)])
    wait_for(send_sem, 4, r_got.at[pl.ds(0, groups - 1)])
    wait_for(send_sem, 5, part_got.at[others])
    wait_for(send_sem, 6, total_got.at[others])


def body(count, groups, saved_input, out_grad, filters, adapter_down, adapter_up):
    width, tokens = saved_input.shape[1], filters.shape[2]
    ranks = adapter_down.shape[0]
    tables = [jnp.asarray(t) for t in make_tables(count)]
    rows = count * CHANS
    hbm = pl.BlockSpec(memory_space=pl.ANY)
    vmem = pl.BlockSpec(memory_space=pltpu.VMEM)
    spec = pltpu.VMEM((rows, 2 * LANES), F32)
    small = pltpu.VMEM((ranks, LANES), F32)
    some = pltpu.VMEM((groups, ranks, LANES), F32)
    tile = pltpu.VMEM((count, 8, LANES), F32)
    narrow = pltpu.VMEM((rows, LANES), BF16)
    wide = pltpu.VMEM((rows, LANES), F32)
    got = pltpu.VMEM((count, CHANS, LANES), BF16)
    grad_input, grad_filter, down, up = pl.pallas_call(
        functools.partial(kernel, count, groups, float(tokens) ** -0.5),
        out_shape=(
            jax.ShapeDtypeStruct((width, LANES), BF16),
            jax.ShapeDtypeStruct((CHANS, tokens), F32),
            jax.ShapeDtypeStruct((ranks, width), F32),
            jax.ShapeDtypeStruct((ranks, width), F32),
        ),
        in_specs=[hbm, hbm, hbm] + [vmem] * 8,
        out_specs=(hbm, hbm, vmem, vmem),
        scratch_shapes=[
            narrow, wide, narrow, narrow, narrow, got, got, narrow, wide, wide, wide,
            spec, spec, small, some, small, some, tile, tile,
            pltpu.VMEM((8, LANES), F32), tile,
            pltpu.SemaphoreType.DMA((5,)),
            pltpu.SemaphoreType.DMA((7,)),
            pltpu.SemaphoreType.DMA((7,)),
        ],
        compiler_params=pltpu.CompilerParams(
            collective_id=0, has_side_effects=True, vmem_limit_bytes=56 * 1024 * 1024
        ),
    )(saved_input[0], out_grad[0], filters[0], adapter_down[:, 0, :], adapter_up[:, 0, :], *tables)
    return grad_input[None], grad_filter[None], down[:, None, :], up[:, None, :]


def solution(mesh):
    placed = (
        P("grp", None, "ctx"),
        P("grp", None, "ctx"),
        P("grp", "ctx", None),
        P(None, "grp", None),
        P(None, "grp", None),
    )
    return jax.shard_map(
        functools.partial(body, mesh.shape["ctx"], mesh.shape["grp"]),
        mesh=mesh,
        in_specs=placed,
        out_specs=(
            P("grp", None, "ctx"),
            P("grp", "ctx", None),
            P(None, "grp", None),
            P(None, "grp", None),
        ),
        check_vma=False,
    )
```

```python
import functools
import math

import jax
import jax.numpy as jnp
import numpy as np
from jax import lax
from jax.experimental import pallas as pl
from jax.experimental.pallas import tpu as pltpu
from jax.sharding import PartitionSpec as P

MESH = pl.DeviceIdType.MESH
F32 = jnp.float32
BF16 = jnp.bfloat16
LANES = 128
CHANS = 32
STEP = 8
CHUNK = 16
CHUNKS = CHANS // CHUNK
EARLY = CHUNKS // 2
DY, U, DU = 4, 4 + CHUNKS, 4 + 2 * CHUNKS
GRID = {64: (4, 4, 2, 2), 8: (2, 2, 1, 2)}
VMEM_LIMIT = 56 * 1024 * 1024
SOURCE = pl.ANY


def halves(table):
    high = table.astype(BF16)
    low = (table - high.astype(np.float64)).astype(BF16)
    return high, low


def make_tables(rows):
    points = 2 * rows * LANES
    n = np.arange(rows)
    p = np.arange(LANES)
    theta = np.outer(n + 0.5, n) * (2.0 * math.pi / (2 * rows))
    phi = np.outer(p, p) * (2.0 * math.pi / LANES)
    turn = np.outer(n + 0.5, p) * (2.0 * math.pi / points)
    high, low = halves(np.concatenate([np.cos(theta), -np.sin(theta)], axis=0))
    first_two = np.concatenate([high, low], axis=1)
    first_three = np.concatenate([high, high, low], axis=1)
    cos, sin = np.cos(phi), np.sin(phi)
    high, low = halves(np.block([[cos, -sin], [sin, cos]]))
    second = np.concatenate([high, high, low], axis=0)
    high, low = halves(np.block([[cos, sin], [-sin, cos]]))
    third = np.concatenate([high, high, low], axis=0)
    high, low = halves(np.concatenate([np.cos(theta).T, -np.sin(theta).T], axis=1) * (2.0 / points))
    last = np.concatenate([high, high, low], axis=1)
    twist = np.stack([np.cos(turn), np.sin(turn)]).astype(np.float32)
    return first_two, first_three, twist, second, third, last


def split(value):
    high = value.astype(BF16)
    return high, (value - high.astype(F32)).astype(BF16)


def dot(left, right, dims=((1,), (0,))):
    return lax.dot_general(left, right, (dims, ((), ())), preferred_element_type=F32)


def gather_rows(ref, first, rows):
    blocks = [ref[pl.ds(first + j, rows, stride=CHANS), :] for j in range(STEP)]
    return jnp.concatenate(blocks, axis=1)


def forward(data, first, twist, second, exact):
    rows = data.shape[0]
    if exact:
        narrow = data.astype(BF16)
        stacked = jnp.concatenate([narrow, narrow], axis=0)
    else:
        high, low = split(data)
        stacked = jnp.concatenate([high, low, high], axis=0)
    part = dot(first[...], stacked)
    cos, sin = twist[0], twist[1]
    joined = []
    for j in range(STEP):
        lanes = slice(j * LANES, (j + 1) * LANES)
        real, imag = part[:rows, lanes], part[rows:, lanes]
        joined.append(jnp.concatenate([real * cos + imag * sin, imag * cos - real * sin], axis=1))
    high, low = split(jnp.concatenate(joined, axis=0))
    return dot(jnp.concatenate([high, low, high], axis=1), second[...])


def inverse(spectrum, twist, third, last):
    rows = twist.shape[1]
    high, low = split(spectrum)
    part = dot(jnp.concatenate([high, low, high], axis=1), third[...])
    cos, sin = twist[0], twist[1]
    reals, imags = [], []
    for j in range(STEP):
        real = part[j * rows : (j + 1) * rows, :LANES]
        imag = part[j * rows : (j + 1) * rows, LANES:]
        reals.append(real * cos - imag * sin)
        imags.append(real * sin + imag * cos)
    joined = jnp.concatenate([jnp.concatenate(reals, axis=1), jnp.concatenate(imags, axis=1)], axis=0)
    high, low = split(joined)
    return dot(last[...], jnp.concatenate([high, low, high], axis=0))


def conj_product(left, right):
    lr, li = left[:, :LANES], left[:, LANES:]
    rr, ri = right[:, :LANES], right[:, LANES:]
    return jnp.concatenate([lr * rr + li * ri, li * rr - lr * ri], axis=1)


def kernel(
    count, groups, factor,
    x_hbm, dy_hbm, h_hbm, a_hbm, b_hbm, first_two_hbm, first_three_hbm, twist_hbm, second_hbm, third_hbm, last_hbm,
    gi_hbm, gf_hbm, gd_hbm, gu_hbm,
    a_ref, b_ref, first_two, first_three, twist, second, third, last,
    x_buf, h_buf, u_buf, du_buf, gi_buf, dy_got, u_got, du_got, wide, work, gf_buf,
    spec_h, spec_dy, z_mine, z_got, r_mine, r_got, parts, part_got, total, total_got,
    load_sem, send_sem, recv_sem,
):
    me = lax.axis_index("ctx")
    grp = lax.axis_index("grp")
    high, wide_x, deep, cores = GRID[count]
    core, near = me % cores, me % (deep * cores) // cores
    place = me // (deep * cores)
    down, across = place // wide_x, place % wide_x
    width = count * CHANS
    ranks = a_ref.shape[0]
    inner = [
        ((near + k // cores) % deep) * cores + (core + k % cores) % cores for k in range(deep * cores)
    ]
    sides = [((near + k) % deep) * cores for k in range(deep)]

    def chip(i):
        return (((down + i // wide_x) % high) * wide_x + (across + i % wide_x) % wide_x) * (deep * cores)

    def each_peer(action):
        for k in range(1, deep * cores):
            action(place * deep * cores + inner[k])

        def run(i, carry):
            base = chip(i)
            for offset in inner:
                action(base + offset)
            return carry

        lax.fori_loop(1, high * wide_x, run, 0)

    def each_owner(role, action):
        @pl.when(core != role)
        def _():
            action(place * deep * cores + sides[0] + role)

        for side in sides[1:]:
            action(place * deep * cores + side + role)

        def run(i, carry):
            base = chip(i)
            for side in sides:
                action(base + side + role)
            return carry

        lax.fori_loop(1, high * wide_x, run, 0)

    def each_group(action):
        for e in range(1, groups):
            action(lax.rem(grp + e, groups))

    def send(src, dst, slot, target):
        pltpu.make_async_remote_copy(
            src_ref=src, dst_ref=dst, send_sem=send_sem.at[slot], recv_sem=recv_sem.at[slot],
            device_id=target, device_id_type=MESH,
        ).start()

    def wait_for(sems, slot, ref):
        pltpu.make_async_copy(ref, ref, sems.at[slot]).wait()

    def rows_of(n, size):
        return pl.ds(pl.multiple_of(n * size, size), size)

    def lanes_of(n):
        return pl.ds(pl.multiple_of(n * LANES, LANES), LANES)

    def chunk_rows(p, q):
        return pl.ds(pl.multiple_of(p * CHANS + q * CHUNK, CHUNK), CHUNK)

    barrier = pltpu.get_barrier_semaphore()

    def greet(target):
        pl.semaphore_signal(barrier, inc=1, device_id=target, device_id_type=MESH)

    each_peer(lambda p: greet({"ctx": p}))
    each_group(lambda g: greet({"grp": g}))

    loads = [
        pltpu.make_async_copy(src, dst, load_sem.at[k])
        for k, (src, dst) in enumerate(
            [
                (a_hbm, a_ref), (x_hbm, x_buf), (first_three_hbm, first_three), (twist_hbm, twist),
                (second_hbm, second), (b_hbm, b_ref), (first_two_hbm, first_two), (third_hbm, third),
                (last_hbm, last),
            ]
        )
    ]
    for load in loads:
        load.start()

    def load_h(n, carry):
        pltpu.make_async_copy(h_hbm.at[:, lanes_of(n)], h_buf.at[rows_of(n, CHANS)], load_sem.at[9]).start()
        return carry

    lax.fori_loop(0, count, load_h, 0)
    own = [
        pltpu.make_async_copy(dy_hbm.at[chunk_rows(me, q)], dy_got.at[q, me], load_sem.at[12 + q])
        for q in range(CHUNKS)
    ]
    for copy in own:
        copy.start()
    loads[0].wait()
    loads[1].wait()
    z_mine[...] = dot(a_ref[...], x_buf[...])
    pl.semaphore_wait(barrier, count - 1 + groups - 1)

    each_group(lambda g: send(z_mine, z_got.at[grp], 0, {"grp": g}))
    for q in range(CHUNKS):
        each_peer(lambda p: send(dy_hbm.at[chunk_rows(p, q)], dy_got.at[q, me], DY + q, {"ctx": p}))

    pltpu.make_async_copy(h_buf, h_buf, load_sem.at[9]).wait()
    for load in loads[2:]:
        load.wait()

    def spectrum_h(i, carry):
        data = gather_rows(h_buf, i * STEP, count)
        spec_h[rows_of(i, STEP * count), :] = forward(data, first_three, twist, second, False)
        return carry

    lax.fori_loop(0, CHANS // STEP, spectrum_h, 0)

    def shared_sum(mine, got):
        got[grp] = mine[...]
        acc = got[0]
        for g in range(1, groups):
            acc = acc + got[g]
        return acc

    def low_rank(base, maps, value, out):
        high_part, low_part = split(value)
        pair = jnp.concatenate([high_part, low_part], axis=0)
        chunk = 256
        for start in range(0, width, chunk):
            left = maps[:, start : start + chunk]
            left = jnp.concatenate([left, left], axis=0)
            extra = dot(left, pair, ((0,), (0,)))
            out[start : start + chunk, :] = (base(start, chunk).astype(F32) + extra).astype(BF16)

    wait_for(recv_sem, 0, z_got.at[pl.ds(0, groups - 1)])
    z = shared_sum(z_mine, z_got)
    low_rank(lambda s, n: x_buf[s : s + n, :], b_ref, z, u_buf)
    for q in range(CHUNKS):
        u_got[q, me] = u_buf[chunk_rows(me, q), :]

    def send_u(q):
        each_peer(lambda p: send(u_buf.at[chunk_rows(p, q)], u_got.at[q, me], U + q, {"ctx": p}))

    for q in range(EARLY):
        send_u(q)

    others = pl.ds(0, count - 1)

    def widen(got, q):
        def run(n, carry):
            wide[chunk_rows(n, q), :] = got[q, n].astype(F32)
            return carry

        lax.fori_loop(0, count, run, 0, unroll=8)

    def scatter_rows(ref, first, value):
        for j in range(STEP):
            ref[pl.ds(first + j, count, stride=CHANS), :] = value[:, j * LANES : (j + 1) * LANES]

    def conv_grad(i, carry):
        rows = rows_of(i, STEP * count)
        spec = forward(gather_rows(wide, i * STEP, count), first_two, twist, second, True)
        spec_dy[rows, :] = spec
        scatter_rows(work, i * STEP, inverse(conj_product(spec, spec_h[rows, :]), twist, third, last))
        return carry

    steps = CHUNK // STEP
    for q in range(CHUNKS):
        own[q].wait()
        wait_for(recv_sem, DY + q, dy_got.at[q, others])
        widen(dy_got, q)
        lax.fori_loop(q * steps, (q + 1) * steps, conv_grad, 0)

        def narrow(n, carry):
            du_buf[chunk_rows(n, q), :] = work[chunk_rows(n, q), :].astype(BF16)
            return carry

        lax.fori_loop(0, count, narrow, 0, unroll=8)
        du_got[chunk_rows(me, q), :] = du_buf[chunk_rows(me, q), :]
        each_peer(lambda p: send(du_buf.at[chunk_rows(p, q)], du_got.at[chunk_rows(me, q)], DU + q, {"ctx": p}))
    for q in range(EARLY, CHUNKS):
        send_u(q)

    def filter_grad(i, carry):
        rows = rows_of(i, STEP * count)
        spec = forward(gather_rows(wide, i * STEP, count), first_two, twist, second, True)
        scatter_rows(gf_buf, i * STEP, inverse(conj_product(spec_dy[rows, :], spec), twist, third, last))
        return carry

    def filter_chunk(q):
        wait_for(recv_sem, U + q, u_got.at[q, others])
        widen(u_got, q)
        lax.fori_loop(q * steps, (q + 1) * steps, filter_grad, 0)

    for q in range(EARLY):
        filter_chunk(q)

    for q in range(CHUNKS):
        wait_for(recv_sem, DU + q, dy_got.at[q, others])
    r_mine[...] = dot(b_ref[...], du_got[...])
    each_group(lambda g: send(r_mine, r_got.at[grp], 1, {"grp": g}))

    blocks = width // LANES
    half = ranks * blocks

    def outer(value, tokens, offset):
        first, rest = split(value)
        both = dot(jnp.concatenate([first, rest], axis=0), tokens, ((1,), (1,)))
        out = (both[:ranks] + both[ranks:]) * factor
        for k in range(blocks):
            parts[pl.ds(offset + k, ranks, stride=blocks), :] = out[:, k * LANES : (k + 1) * LANES]

    def tile_of(p):
        return rows_of(p % 2 * (count // 2) + p // 2, 8)

    def send_parts(role):
        each_owner(role, lambda p: send(parts.at[tile_of(p)], part_got.at[me], 2, {"ctx": p}))

    outer(z, du_got[...], half)
    send_parts(1)
    wait_for(recv_sem, 1, r_got.at[pl.ds(0, groups - 1)])
    rank_grad = shared_sum(r_mine, r_got)
    outer(rank_grad, x_buf[...], 0)
    send_parts(0)
    part_got[me] = parts[tile_of(me), :]
    low_rank(lambda s, n: du_got[s : s + n, :], a_ref, rank_grad, gi_buf)
    gi_store = pltpu.make_async_copy(gi_buf, gi_hbm, load_sem.at[10])
    gi_store.start()

    for q in range(EARLY, CHUNKS):
        filter_chunk(q)

    def store_gf(n, carry):
        pltpu.make_async_copy(gf_buf.at[rows_of(n, CHANS)], gf_hbm.at[:, lanes_of(n)], load_sem.at[11]).start()
        return carry

    lax.fori_loop(0, count, store_gf, 0)

    wait_for(recv_sem, 2, part_got.at[others])
    acc = jnp.sum(part_got[...], axis=0)
    total[...] = acc
    total_got[tile_of(me), :] = acc
    each_peer(lambda p: send(total, total_got.at[tile_of(me)], 3, {"ctx": p}))
    wait_for(recv_sem, 3, part_got.at[others])
    stores = [
        pltpu.make_async_copy(total_got.at[pl.ds(0, half)], gd_hbm, load_sem.at[0]),
        pltpu.make_async_copy(total_got.at[pl.ds(half, half)], gu_hbm, load_sem.at[1]),
    ]
    for store in stores:
        store.start()

    gi_store.wait()
    pltpu.make_async_copy(gf_buf, gf_buf, load_sem.at[11]).wait()
    for slot in range(2):
        wait_for(send_sem, slot, z_got.at[pl.ds(0, groups - 1)])
    for slot in range(2, 4):
        wait_for(send_sem, slot, part_got.at[others])
    for slot in range(DY, DY + 3 * CHUNKS):
        wait_for(send_sem, slot, dy_got.at[0, others])
    for store in stores:
        store.wait()


def body(count, groups, saved_input, out_grad, filters, adapter_down, adapter_up):
    width, tokens = saved_input.shape[1], filters.shape[2]
    ranks = adapter_down.shape[0]
    tables = [jnp.asarray(t) for t in make_tables(count)]
    rows = count * CHANS
    hbm = pl.BlockSpec(memory_space=pl.ANY)
    source = pl.BlockSpec(memory_space=SOURCE)
    spec = pltpu.VMEM((rows, 2 * LANES), F32)
    small = pltpu.VMEM((ranks, LANES), F32)
    some = pltpu.VMEM((groups, ranks, LANES), F32)
    narrow = pltpu.VMEM((rows, LANES), BF16)
    wide = pltpu.VMEM((rows, LANES), F32)
    maps = pltpu.VMEM((ranks, width), BF16)
    tiles = pltpu.VMEM((count * 8, LANES), F32)
    got = pltpu.VMEM((CHUNKS, count, CHUNK, LANES), BF16)
    flat = ranks * width // LANES
    grad_input, grad_filter, down, up = pl.pallas_call(
        functools.partial(kernel, count, groups, float(tokens) ** -0.5),
        out_shape=(
            jax.ShapeDtypeStruct((width, LANES), BF16),
            jax.ShapeDtypeStruct((CHANS, tokens), F32),
            jax.ShapeDtypeStruct((flat, LANES), F32),
            jax.ShapeDtypeStruct((flat, LANES), F32),
        ),
        in_specs=[source] * 11,
        out_specs=(hbm,) * 4,
        scratch_shapes=[
            maps, maps, *[pltpu.VMEM(t.shape, t.dtype) for t in tables],
            narrow, wide, narrow, narrow, narrow, got, got, narrow, wide, wide, wide,
            spec, spec, small, some, small, some, tiles, pltpu.VMEM((count, 8, LANES), F32),
            pltpu.VMEM((8, LANES), F32), tiles,
            pltpu.SemaphoreType.DMA((12 + CHUNKS,)),
            pltpu.SemaphoreType.DMA((4 + 3 * CHUNKS,)),
            pltpu.SemaphoreType.DMA((4 + 3 * CHUNKS,)),
        ],
        compiler_params=pltpu.CompilerParams(
            collective_id=0, has_side_effects=True, vmem_limit_bytes=VMEM_LIMIT
        ),
    )(saved_input[0], out_grad[0], filters[0], adapter_down[:, 0, :], adapter_up[:, 0, :], *tables)
    return (
        grad_input[None],
        grad_filter[None],
        down.reshape(ranks, 1, width),
        up.reshape(ranks, 1, width),
    )


def solution(mesh):
    placed = (
        P("grp", None, "ctx"),
        P("grp", None, "ctx"),
        P("grp", "ctx", None),
        P(None, "grp", None),
        P(None, "grp", None),
    )
    return jax.shard_map(
        functools.partial(body, mesh.shape["ctx"], mesh.shape["grp"]),
        mesh=mesh,
        in_specs=placed,
        out_specs=(
            P("grp", None, "ctx"),
            P("grp", "ctx", None),
            P(None, "grp", None),
            P(None, "grp", None),
        ),
        check_vma=False,
    )
```

```python
import functools
import math

import jax
import jax.numpy as jnp
import numpy as np
from jax import lax
from jax.experimental import pallas as pl
from jax.experimental.pallas import tpu as pltpu
from jax.sharding import PartitionSpec as P

MESH = pl.DeviceIdType.MESH
F32 = jnp.float32
BF16 = jnp.bfloat16
LANES = 128
CHANS = 32
STEP = 8
CHUNK = 16
CHUNKS = CHANS // CHUNK
EARLY = CHUNKS // 2
FAR = True
DY, U, DU = 4, 4 + CHUNKS, 4 + 2 * CHUNKS
GRID = {64: (4, 4, 2, 2), 8: (2, 2, 1, 2)}
VMEM_LIMIT = 56 * 1024 * 1024
SOURCE = pl.ANY


def far_first(high, wide, direct):
    def hops(i):
        down, across = i // wide, i % wide
        return min(down, high - down) + min(across, wide - across)

    order = sorted(range(1, high * wide), key=lambda i: (-hops(i), i) if direct else i)
    late = [k for k, i in enumerate(order[:8]) if i < 8]
    if len(order) > 8:
        order.insert(7, order.pop(late[-1]))
    codes = [sum(i << (4 * k) for k, i in enumerate(part)) for part in (order[:8], order[8:])]
    return len(order), codes


def halves(table):
    high = table.astype(BF16)
    low = (table - high.astype(np.float64)).astype(BF16)
    return high, low


def make_tables(rows):
    points = 2 * rows * LANES
    n = np.arange(rows)
    p = np.arange(LANES)
    theta = np.outer(n + 0.5, n) * (2.0 * math.pi / (2 * rows))
    phi = np.outer(p, p) * (2.0 * math.pi / LANES)
    turn = np.outer(n + 0.5, p) * (2.0 * math.pi / points)
    high, low = halves(np.concatenate([np.cos(theta), -np.sin(theta)], axis=0))
    first_two = np.concatenate([high, low], axis=1)
    first_three = np.concatenate([high, high, low], axis=1)
    cos, sin = np.cos(phi), np.sin(phi)
    high, low = halves(np.block([[cos, -sin], [sin, cos]]))
    second = np.concatenate([high, high, low], axis=0)
    high, low = halves(np.block([[cos, sin], [-sin, cos]]))
    third = np.concatenate([high, high, low], axis=0)
    high, low = halves(np.concatenate([np.cos(theta).T, -np.sin(theta).T], axis=1) * (2.0 / points))
    last = np.concatenate([high, high, low], axis=1)
    twist = np.stack([np.cos(turn), np.sin(turn)]).astype(np.float32)
    return first_two, first_three, twist, second, third, last


def split(value):
    high = value.astype(BF16)
    return high, (value - high.astype(F32)).astype(BF16)


def dot(left, right, dims=((1,), (0,))):
    return lax.dot_general(left, right, (dims, ((), ())), preferred_element_type=F32)


def gather_rows(ref, first, rows):
    blocks = [ref[pl.ds(first + j, rows, stride=CHANS), :] for j in range(STEP)]
    return jnp.concatenate(blocks, axis=1)


def forward(data, first, twist, second, exact):
    rows = data.shape[0]
    if exact:
        narrow = data.astype(BF16)
        stacked = jnp.concatenate([narrow, narrow], axis=0)
    else:
        high, low = split(data)
        stacked = jnp.concatenate([high, low, high], axis=0)
    part = dot(first[...], stacked)
    cos, sin = twist[0], twist[1]
    joined = []
    for j in range(STEP):
        lanes = slice(j * LANES, (j + 1) * LANES)
        real, imag = part[:rows, lanes], part[rows:, lanes]
        joined.append(jnp.concatenate([real * cos + imag * sin, imag * cos - real * sin], axis=1))
    high, low = split(jnp.concatenate(joined, axis=0))
    return dot(jnp.concatenate([high, low, high], axis=1), second[...])


def inverse(spectrum, twist, third, last):
    rows = twist.shape[1]
    high, low = split(spectrum)
    part = dot(jnp.concatenate([high, low, high], axis=1), third[...])
    cos, sin = twist[0], twist[1]
    reals, imags = [], []
    for j in range(STEP):
        real = part[j * rows : (j + 1) * rows, :LANES]
        imag = part[j * rows : (j + 1) * rows, LANES:]
        reals.append(real * cos - imag * sin)
        imags.append(real * sin + imag * cos)
    joined = jnp.concatenate([jnp.concatenate(reals, axis=1), jnp.concatenate(imags, axis=1)], axis=0)
    high, low = split(joined)
    return dot(last[...], jnp.concatenate([high, low, high], axis=0))


def conj_product(left, right):
    lr, li = left[:, :LANES], left[:, LANES:]
    rr, ri = right[:, :LANES], right[:, LANES:]
    return jnp.concatenate([lr * rr + li * ri, li * rr - lr * ri], axis=1)


def kernel(
    count, groups, factor,
    x_hbm, dy_hbm, h_hbm, a_hbm, b_hbm, first_two_hbm, first_three_hbm, twist_hbm, second_hbm, third_hbm, last_hbm,
    gi_ref, gf_ref, gd_ref, gu_ref,
    a_ref, b_ref, first_two, first_three, twist, second, third, last,
    x_buf, h_buf, u_buf, du_buf, dy_got, u_got, du_got, wide, work, gf_buf,
    spec_h, spec_dy, z_mine, z_got, r_mine, r_got, parts, part_got, total, total_got,
    load_sem, send_sem, recv_sem,
):
    me = lax.axis_index("ctx")
    grp = lax.axis_index("grp")
    high, wide_x, deep, cores = GRID[count]
    core, near = me % cores, me % (deep * cores) // cores
    place = me // (deep * cores)
    down, across = place // wide_x, place % wide_x
    chips, codes = far_first(high, wide_x, FAR)
    width = count * CHANS
    ranks = a_ref.shape[0]
    inner = [
        ((near + k // cores) % deep) * cores + (core + k % cores) % cores
        for k in reversed(range(deep * cores))
    ]
    sides = [((near + k) % deep) * cores for k in reversed(range(deep))]

    def chip(t):
        code = jnp.where(t < 8, codes[0], codes[1])
        i = (code >> (4 * (t & 7))) & 15
        row = (down + i // wide_x if wide_x != 4 else down + (i >> 2)) & (high - 1)
        column = (across + i) & (wide_x - 1)
        return (row * wide_x + column) * (deep * cores)

    def each_peer(action):
        def run(t, carry):
            base = chip(t)
            for offset in inner:
                action(base + offset)
            return carry

        lax.fori_loop(0, chips, run, 0)
        for offset in inner[:-1]:
            action(place * deep * cores + offset)

    def each_owner(role, action):
        def run(t, carry):
            base = chip(t)
            for side in sides:
                action(base + side + role)
            return carry

        lax.fori_loop(0, chips, run, 0)
        for side in sides[:-1]:
            action(place * deep * cores + side + role)

        @pl.when(core != role)
        def _():
            action(place * deep * cores + sides[-1] + role)

    def each_group(action):
        for e in range(1, groups):
            action(lax.rem(grp + e, groups))

    def send(src, dst, slot, target):
        pltpu.make_async_remote_copy(
            src_ref=src, dst_ref=dst, send_sem=send_sem.at[slot], recv_sem=recv_sem.at[slot],
            device_id=target, device_id_type=MESH,
        ).start()

    def wait_for(sems, slot, ref):
        pltpu.make_async_copy(ref, ref, sems.at[slot]).wait()

    def rows_of(n, size):
        return pl.ds(pl.multiple_of(n * size, size), size)

    def lanes_of(n):
        return pl.ds(pl.multiple_of(n * LANES, LANES), LANES)

    def chunk_rows(p, q):
        return pl.ds(pl.multiple_of(p * CHANS + q * CHUNK, CHUNK), CHUNK)

    barrier = pltpu.get_barrier_semaphore()

    def greet(target):
        pl.semaphore_signal(barrier, inc=1, device_id=target, device_id_type=MESH)

    each_peer(lambda p: greet({"ctx": p}))
    each_group(lambda g: greet({"grp": g}))

    loads = [
        pltpu.make_async_copy(src, dst, load_sem.at[k])
        for k, (src, dst) in enumerate(
            [
                (a_hbm, a_ref), (x_hbm, x_buf), (first_three_hbm, first_three), (twist_hbm, twist),
                (second_hbm, second), (b_hbm, b_ref), (first_two_hbm, first_two), (third_hbm, third),
                (last_hbm, last),
            ]
        )
    ]
    for load in loads:
        load.start()

    def load_h(n, carry):
        pltpu.make_async_copy(h_hbm.at[:, lanes_of(n)], h_buf.at[rows_of(n, CHANS)], load_sem.at[9]).start()
        return carry

    lax.fori_loop(0, count, load_h, 0)
    own = [
        pltpu.make_async_copy(dy_hbm.at[chunk_rows(me, q)], dy_got.at[q, me], load_sem.at[12 + q])
        for q in range(CHUNKS)
    ]
    for copy in own:
        copy.start()
    loads[0].wait()
    loads[1].wait()
    z_mine[...] = dot(a_ref[...], x_buf[...])
    pl.semaphore_wait(barrier, count - 1 + groups - 1)

    each_group(lambda g: send(z_mine, z_got.at[grp], 0, {"grp": g}))
    for q in range(CHUNKS):
        each_peer(lambda p: send(dy_hbm.at[chunk_rows(p, q)], dy_got.at[q, me], DY + q, {"ctx": p}))

    pltpu.make_async_copy(h_buf, h_buf, load_sem.at[9]).wait()
    for load in loads[2:]:
        load.wait()

    def spectrum_h(i, carry):
        data = gather_rows(h_buf, i * STEP, count)
        spec_h[rows_of(i, STEP * count), :] = forward(data, first_three, twist, second, False)
        return carry

    lax.fori_loop(0, CHANS // STEP, spectrum_h, 0)

    def shared_sum(mine, got):
        got[grp] = mine[...]
        acc = got[0]
        for g in range(1, groups):
            acc = acc + got[g]
        return acc

    def low_rank(base, maps, value, out):
        high_part, low_part = split(value)
        pair = jnp.concatenate([high_part, low_part], axis=0)
        chunk = 256
        for start in range(0, width, chunk):
            left = maps[:, start : start + chunk]
            left = jnp.concatenate([left, left], axis=0)
            extra = dot(left, pair, ((0,), (0,)))
            out[start : start + chunk, :] = (base(start, chunk).astype(F32) + extra).astype(BF16)

    wait_for(recv_sem, 0, z_got.at[pl.ds(0, groups - 1)])
    z = shared_sum(z_mine, z_got)
    low_rank(lambda s, n: x_buf[s : s + n, :], b_ref, z, u_buf)
    for q in range(CHUNKS):
        u_got[q, me] = u_buf[chunk_rows(me, q), :]

    def send_u(q):
        each_peer(lambda p: send(u_buf.at[chunk_rows(p, q)], u_got.at[q, me], U + q, {"ctx": p}))

    for q in range(EARLY):
        send_u(q)

    others = pl.ds(0, count - 1)

    def widen(got, q):
        def run(n, carry):
            wide[chunk_rows(n, q), :] = got[q, n].astype(F32)
            return carry

        lax.fori_loop(0, count, run, 0, unroll=8)

    def scatter_rows(ref, first, value):
        for j in range(STEP):
            ref[pl.ds(first + j, count, stride=CHANS), :] = value[:, j * LANES : (j + 1) * LANES]

    def conv_grad(i, carry):
        rows = rows_of(i, STEP * count)
        spec = forward(gather_rows(wide, i * STEP, count), first_two, twist, second, True)
        spec_dy[rows, :] = spec
        scatter_rows(work, i * STEP, inverse(conj_product(spec, spec_h[rows, :]), twist, third, last))
        return carry

    steps = CHUNK // STEP
    for q in range(CHUNKS):
        own[q].wait()
        wait_for(recv_sem, DY + q, dy_got.at[q, others])
        widen(dy_got, q)
        lax.fori_loop(q * steps, (q + 1) * steps, conv_grad, 0)

        def narrow(n, carry):
            du_buf[chunk_rows(n, q), :] = work[chunk_rows(n, q), :].astype(BF16)
            return carry

        lax.fori_loop(0, count, narrow, 0, unroll=8)
        du_got[chunk_rows(me, q), :] = du_buf[chunk_rows(me, q), :]
        each_peer(lambda p: send(du_buf.at[chunk_rows(p, q)], du_got.at[chunk_rows(me, q)], DU + q, {"ctx": p}))
    for q in range(EARLY, CHUNKS):
        send_u(q)

    def filter_grad(i, carry):
        rows = rows_of(i, STEP * count)
        spec = forward(gather_rows(wide, i * STEP, count), first_two, twist, second, True)
        scatter_rows(gf_buf, i * STEP, inverse(conj_product(spec_dy[rows, :], spec), twist, third, last))
        return carry

    def filter_chunk(q):
        wait_for(recv_sem, U + q, u_got.at[q, others])
        widen(u_got, q)
        lax.fori_loop(q * steps, (q + 1) * steps, filter_grad, 0)

    for q in range(EARLY):
        filter_chunk(q)

    for q in range(CHUNKS):
        wait_for(recv_sem, DU + q, dy_got.at[q, others])
    r_mine[...] = dot(b_ref[...], du_got[...])
    each_group(lambda g: send(r_mine, r_got.at[grp], 1, {"grp": g}))

    blocks = width // LANES
    half = ranks * blocks

    def outer(value, tokens, offset):
        first, rest = split(value)
        both = dot(jnp.concatenate([first, rest], axis=0), tokens, ((1,), (1,)))
        out = (both[:ranks] + both[ranks:]) * factor
        for k in range(blocks):
            parts[pl.ds(offset + k, ranks, stride=blocks), :] = out[:, k * LANES : (k + 1) * LANES]

    def tile_of(p):
        return rows_of(p % 2 * (count // 2) + p // 2, 8)

    def send_parts(role):
        each_owner(role, lambda p: send(parts.at[tile_of(p)], part_got.at[me], 2, {"ctx": p}))

    outer(z, du_got[...], half)
    send_parts(1)
    wait_for(recv_sem, 1, r_got.at[pl.ds(0, groups - 1)])
    rank_grad = shared_sum(r_mine, r_got)
    outer(rank_grad, x_buf[...], 0)
    send_parts(0)
    part_got[me] = parts[tile_of(me), :]
    low_rank(lambda s, n: du_got[s : s + n, :], a_ref, rank_grad, gi_ref)

    for q in range(EARLY, CHUNKS):
        filter_chunk(q)
    wait_for(recv_sem, 2, part_got.at[others])
    acc = jnp.sum(part_got[...], axis=0)
    total[...] = acc
    total_got[tile_of(me), :] = acc
    each_peer(lambda p: send(total, total_got.at[tile_of(me)], 3, {"ctx": p}))

    def store_gf(n, carry):
        pltpu.make_async_copy(gf_buf.at[rows_of(n, CHANS)], gf_ref.at[:, lanes_of(n)], load_sem.at[11]).start()
        return carry

    lax.fori_loop(0, count, store_gf, 0)

    wait_for(recv_sem, 3, part_got.at[others])
    gd_ref[...] = total_got[pl.ds(0, half), :]
    gu_ref[...] = total_got[pl.ds(half, half), :]

    pltpu.make_async_copy(gf_buf, gf_buf, load_sem.at[11]).wait()
    for slot in range(2):
        wait_for(send_sem, slot, z_got.at[pl.ds(0, groups - 1)])
    for slot in range(2, 4):
        wait_for(send_sem, slot, part_got.at[others])
    for slot in range(DY, DY + 3 * CHUNKS):
        wait_for(send_sem, slot, dy_got.at[0, others])


def store_kernel(gi, gf, gd, gu, gi_out, gf_out, gd_out, gu_out, sems):
    copies = [
        pltpu.make_async_copy(src, dst, sems.at[k])
        for k, (src, dst) in enumerate([(gf, gf_out), (gi, gi_out), (gd, gd_out), (gu, gu_out)])
    ]
    for copy in copies:
        copy.start()
    for copy in copies:
        copy.wait()


def body(count, groups, saved_input, out_grad, filters, adapter_down, adapter_up):
    width, tokens = saved_input.shape[1], filters.shape[2]
    ranks = adapter_down.shape[0]
    tables = [jnp.asarray(t) for t in make_tables(count)]
    rows = count * CHANS
    hbm = pl.BlockSpec(memory_space=pl.ANY)
    source = pl.BlockSpec(memory_space=SOURCE)
    spec = pltpu.VMEM((rows, 2 * LANES), F32)
    small = pltpu.VMEM((ranks, LANES), F32)
    some = pltpu.VMEM((groups, ranks, LANES), F32)
    narrow = pltpu.VMEM((rows, LANES), BF16)
    wide = pltpu.VMEM((rows, LANES), F32)
    maps = pltpu.VMEM((ranks, width), BF16)
    tiles = pltpu.VMEM((count * 8, LANES), F32)
    got = pltpu.VMEM((CHUNKS, count, CHUNK, LANES), BF16)
    flat = ranks * width // LANES
    results = pl.pallas_call(
        functools.partial(kernel, count, groups, float(tokens) ** -0.5),
        out_shape=(
            pltpu.VMEM((width, LANES), BF16),
            pltpu.VMEM((CHANS, tokens), F32),
            pltpu.VMEM((flat, LANES), F32),
            pltpu.VMEM((flat, LANES), F32),
        ),
        in_specs=[source] * 11,
        out_specs=(pl.BlockSpec(memory_space=pltpu.VMEM),) * 4,
        scratch_shapes=[
            maps, maps, *[pltpu.VMEM(t.shape, t.dtype) for t in tables],
            narrow, wide, narrow, narrow, got, got, narrow, wide, wide, wide,
            spec, spec, small, some, small, some, tiles, pltpu.VMEM((count, 8, LANES), F32),
            pltpu.VMEM((8, LANES), F32), tiles,
            pltpu.SemaphoreType.DMA((12 + CHUNKS,)),
            pltpu.SemaphoreType.DMA((4 + 3 * CHUNKS,)),
            pltpu.SemaphoreType.DMA((4 + 3 * CHUNKS,)),
        ],
        compiler_params=pltpu.CompilerParams(
            collective_id=0, has_side_effects=True, vmem_limit_bytes=VMEM_LIMIT
        ),
    )(saved_input[0], out_grad[0], filters[0], adapter_down[:, 0, :], adapter_up[:, 0, :], *tables)
    grad_input, grad_filter, down, up = pl.pallas_call(
        store_kernel,
        out_shape=tuple(jax.ShapeDtypeStruct(r.shape, r.dtype) for r in results),
        in_specs=[pl.BlockSpec(memory_space=pltpu.VMEM)] * 4,
        out_specs=(hbm,) * 4,
        scratch_shapes=[pltpu.SemaphoreType.DMA((4,))],
    )(*[pltpu.with_memory_space_constraint(r, pltpu.VMEM) for r in results])
    return (
        grad_input[None],
        grad_filter[None],
        down.reshape(ranks, 1, width),
        up.reshape(ranks, 1, width),
    )


def solution(mesh):
    placed = (
        P("grp", None, "ctx"),
        P("grp", None, "ctx"),
        P("grp", "ctx", None),
        P(None, "grp", None),
        P(None, "grp", None),
    )
    return jax.shard_map(
        functools.partial(body, mesh.shape["ctx"], mesh.shape["grp"]),
        mesh=mesh,
        in_specs=placed,
        out_specs=(
            P("grp", None, "ctx"),
            P("grp", "ctx", None),
            P(None, "grp", None),
            P(None, "grp", None),
        ),
        check_vma=False,
    )
```

```python
import functools
import math

import jax
import jax.numpy as jnp
import numpy as np
from jax import lax
from jax.experimental import pallas as pl
from jax.experimental.pallas import tpu as pltpu
from jax.sharding import PartitionSpec as P

MESH = pl.DeviceIdType.MESH
F32 = jnp.float32
BF16 = jnp.bfloat16
LANES = 128
CHANS = 32
STEP = 16
CHUNK = 16
CHUNKS = CHANS // CHUNK
SENDS = (1, 0, 1)
FILLS = (1, 1, 0)
GROUP_ORDER = (1, 2, 3)
FAR = True
DY, U, DU = 4, 4 + CHUNKS, 4 + 2 * CHUNKS
GRID = {64: (4, 4, 2, 2), 8: (2, 2, 1, 2)}
VMEM_LIMIT = 56 * 1024 * 1024
SOURCE = pl.ANY


def far_first(high, wide, direct):
    def hops(i):
        down, across = i // wide, i % wide
        return min(down, high - down) + min(across, wide - across)

    order = sorted(range(1, high * wide), key=lambda i: (-hops(i), i) if direct else i)
    late = [k for k, i in enumerate(order[:8]) if i < 8]
    if len(order) > 8:
        order.insert(7, order.pop(late[-1]))
    codes = [sum(i << (4 * k) for k, i in enumerate(part)) for part in (order[:8], order[8:])]
    return len(order), codes


def halves(table):
    high = table.astype(BF16)
    low = (table - high.astype(np.float64)).astype(BF16)
    return high, low


def make_tables(rows):
    points = 2 * rows * LANES
    n = np.arange(rows)
    p = np.arange(LANES)
    theta = np.outer(n + 0.5, n) * (2.0 * math.pi / (2 * rows))
    phi = np.outer(p, p) * (2.0 * math.pi / LANES)
    turn = np.outer(n + 0.5, p) * (2.0 * math.pi / points)
    high, low = halves(np.concatenate([np.cos(theta), -np.sin(theta)], axis=0))
    first_two = np.concatenate([high, low], axis=1)
    first_three = np.concatenate([high, high, low], axis=1)
    cos, sin = np.cos(phi), np.sin(phi)
    high, low = halves(np.block([[cos, -sin], [sin, cos]]))
    second = np.concatenate([high, high, low], axis=0)
    high, low = halves(np.block([[cos, sin], [-sin, cos]]))
    third = np.concatenate([high, high, low], axis=0)
    high, low = halves(np.concatenate([np.cos(theta).T, -np.sin(theta).T], axis=1) * (2.0 / points))
    last = np.concatenate([high, high, low], axis=1)
    twist = np.stack([np.cos(turn), np.sin(turn)]).astype(np.float32)
    return first_two, first_three, twist, second, third, last


def split(value):
    high = value.astype(BF16)
    return high, (value - high.astype(F32)).astype(BF16)


def dot(left, right, dims=((1,), (0,))):
    return lax.dot_general(left, right, (dims, ((), ())), preferred_element_type=F32)


def gather_rows(ref, first, rows):
    block = ref[:, pl.ds(pl.multiple_of(first, STEP), STEP), :].astype(F32)
    turned = jnp.swapaxes(block, 0, 1)
    return jnp.concatenate([turned[j] for j in range(STEP)], axis=1)


def forward(data, first, twist, second, exact):
    rows = data.shape[0]
    if exact:
        narrow = data.astype(BF16)
        stacked = jnp.concatenate([narrow, narrow], axis=0)
    else:
        high, low = split(data)
        stacked = jnp.concatenate([high, low, high], axis=0)
    part = dot(first[...], stacked)
    cos, sin = twist[0], twist[1]
    joined = []
    for j in range(STEP):
        lanes = slice(j * LANES, (j + 1) * LANES)
        real, imag = part[:rows, lanes], part[rows:, lanes]
        joined.append(jnp.concatenate([real * cos + imag * sin, imag * cos - real * sin], axis=1))
    high, low = split(jnp.concatenate(joined, axis=0))
    return dot(jnp.concatenate([high, low, high], axis=1), second[...])


def inverse(spectrum, twist, third, last):
    rows = twist.shape[1]
    high, low = split(spectrum)
    part = dot(jnp.concatenate([high, low, high], axis=1), third[...])
    cos, sin = twist[0], twist[1]
    reals, imags = [], []
    for j in range(STEP):
        real = part[j * rows : (j + 1) * rows, :LANES]
        imag = part[j * rows : (j + 1) * rows, LANES:]
        reals.append(real * cos - imag * sin)
        imags.append(real * sin + imag * cos)
    joined = jnp.concatenate([jnp.concatenate(reals, axis=1), jnp.concatenate(imags, axis=1)], axis=0)
    high, low = split(joined)
    return dot(last[...], jnp.concatenate([high, low, high], axis=0))


def conj_product(left, right):
    lr, li = left[:, :LANES], left[:, LANES:]
    rr, ri = right[:, :LANES], right[:, LANES:]
    return jnp.concatenate([lr * rr + li * ri, li * rr - lr * ri], axis=1)


def kernel(
    count, groups, factor,
    x_hbm, dy_hbm, h_hbm, a_hbm, b_hbm, first_two_hbm, first_three_hbm, twist_hbm, second_hbm, third_hbm, last_hbm,
    gi_ref, gf_ref, gd_ref, gu_ref,
    a_ref, b_ref, first_two, first_three, twist, second, third, last,
    x_buf, h_buf, u_buf, du_buf, dy_got, u_got, du_got, work, gf_buf,
    spec_h, spec_dy, z_mine, z_got, r_mine, r_got, parts, part_got, total, total_got,
    load_sem, send_sem, recv_sem,
):
    me = lax.axis_index("ctx")
    grp = lax.axis_index("grp")
    high, wide_x, deep, cores = GRID[count]
    core, near = me % cores, me % (deep * cores) // cores
    place = me // (deep * cores)
    down, across = place // wide_x, place % wide_x
    chips, codes = far_first(high, wide_x, FAR)
    width = count * CHANS
    ranks = a_ref.shape[0]
    inner = [
        ((near + k // cores) % deep) * cores + (core + k % cores) % cores
        for k in reversed(range(deep * cores))
    ]
    sides = [((near + k) % deep) * cores for k in reversed(range(deep))]

    def chip(t):
        code = jnp.where(t < 8, codes[0], codes[1])
        i = (code >> (4 * (t & 7))) & 15
        row = (down + i // wide_x if wide_x != 4 else down + (i >> 2)) & (high - 1)
        column = (across + i) & (wide_x - 1)
        return (row * wide_x + column) * (deep * cores)

    def each_peer(action):
        def run(t, carry):
            base = chip(t)
            for offset in inner:
                action(base + offset)
            return carry

        lax.fori_loop(0, chips, run, 0)
        for offset in inner[:-1]:
            action(place * deep * cores + offset)

    def each_owner(role, action):
        def run(t, carry):
            base = chip(t)
            for side in sides:
                action(base + side + role)
            return carry

        lax.fori_loop(0, chips, run, 0)
        for side in sides[:-1]:
            action(place * deep * cores + side + role)

        @pl.when(core != role)
        def _():
            action(place * deep * cores + sides[-1] + role)

    def each_group(action):
        for e in GROUP_ORDER:
            if e < groups:
                action(lax.rem(grp + e, groups))

    def send(src, dst, slot, target):
        pltpu.make_async_remote_copy(
            src_ref=src, dst_ref=dst, send_sem=send_sem.at[slot], recv_sem=recv_sem.at[slot],
            device_id=target, device_id_type=MESH,
        ).start()

    def wait_for(sems, slot, ref):
        pltpu.make_async_copy(ref, ref, sems.at[slot]).wait()

    def rows_of(n, size):
        return pl.ds(pl.multiple_of(n * size, size), size)

    def lanes_of(n):
        return pl.ds(pl.multiple_of(n * LANES, LANES), LANES)

    def chunk_rows(p, q):
        return pl.ds(pl.multiple_of(p * CHANS + q * CHUNK, CHUNK), CHUNK)

    barrier = pltpu.get_barrier_semaphore()

    def greet(target):
        pl.semaphore_signal(barrier, inc=1, device_id=target, device_id_type=MESH)

    each_peer(lambda p: greet({"ctx": p}))
    each_group(lambda g: greet({"grp": g}))

    loads = [
        pltpu.make_async_copy(src, dst, load_sem.at[k])
        for k, (src, dst) in enumerate(
            [
                (a_hbm, a_ref), (x_hbm, x_buf), (first_three_hbm, first_three), (twist_hbm, twist),
                (second_hbm, second), (b_hbm, b_ref), (first_two_hbm, first_two), (third_hbm, third),
                (last_hbm, last),
            ]
        )
    ]
    for load in loads:
        load.start()

    def load_h(n, carry):
        pltpu.make_async_copy(h_hbm.at[:, lanes_of(n)], h_buf.at[n], load_sem.at[9]).start()
        return carry

    lax.fori_loop(0, count, load_h, 0)
    own = [
        pltpu.make_async_copy(dy_hbm.at[chunk_rows(me, q)], dy_got.at[q, me], load_sem.at[12 + q])
        for q in range(CHUNKS)
    ]
    for copy in own:
        copy.start()
    loads[0].wait()
    loads[1].wait()
    z_mine[...] = dot(a_ref[...], x_buf[...])
    pl.semaphore_wait(barrier, count - 1 + groups - 1)

    each_group(lambda g: send(z_mine, z_got.at[grp], 0, {"grp": g}))
    for q in range(CHUNKS):
        each_peer(lambda p: send(dy_hbm.at[chunk_rows(p, q)], dy_got.at[q, me], DY + q, {"ctx": p}))

    pltpu.make_async_copy(h_buf, h_buf, load_sem.at[9]).wait()
    for load in loads[2:]:
        load.wait()

    def spectrum_h(i, carry):
        data = gather_rows(h_buf, i * STEP, count)
        spec_h[rows_of(i, STEP * count), :] = forward(data, first_three, twist, second, False)
        return carry

    lax.fori_loop(0, CHANS // STEP, spectrum_h, 0)

    def shared_sum(mine, got):
        got[grp] = mine[...]
        acc = got[0]
        for g in range(1, groups):
            acc = acc + got[g]
        return acc

    def low_rank(base, maps, value, out):
        high_part, low_part = split(value)
        pair = jnp.concatenate([high_part, low_part], axis=0)
        chunk = 256
        for start in range(0, width, chunk):
            left = maps[:, start : start + chunk]
            left = jnp.concatenate([left, left], axis=0)
            extra = dot(left, pair, ((0,), (0,)))
            out[start : start + chunk, :] = (base(start, chunk).astype(F32) + extra).astype(BF16)

    wait_for(recv_sem, 0, z_got.at[pl.ds(0, groups - 1)])
    z = shared_sum(z_mine, z_got)
    low_rank(lambda s, n: x_buf[s : s + n, :], b_ref, z, u_buf)
    for q in range(CHUNKS):
        u_got[q, me] = u_buf[chunk_rows(me, q), :]

    def send_u(q):
        each_peer(lambda p: send(u_buf.at[chunk_rows(p, q)], u_got.at[q, me], U + q, {"ctx": p}))

    pending = list(range(CHUNKS))

    def send_some(position):
        for _ in range(SENDS[position]):
            send_u(pending.pop(0))

    send_some(0)

    others = pl.ds(0, count - 1)

    def scatter_rows(ref, first, value):
        turned = jnp.stack([value[:, j * LANES : (j + 1) * LANES] for j in range(STEP)])
        ref[:, pl.ds(pl.multiple_of(first, STEP), STEP), :] = jnp.swapaxes(turned, 0, 1)

    def conv_grad(q, i, carry):
        rows = rows_of(i, STEP * count)
        spec = forward(gather_rows(dy_got.at[q], (i - q * steps) * STEP, count), first_two, twist, second, True)
        spec_dy[rows, :] = spec
        scatter_rows(work, i * STEP, inverse(conj_product(spec, spec_h[rows, :]), twist, third, last))
        return carry

    steps = CHUNK // STEP
    for q in range(CHUNKS):
        own[q].wait()
        wait_for(recv_sem, DY + q, dy_got.at[q, others])
        lax.fori_loop(q * steps, (q + 1) * steps, functools.partial(conv_grad, q), 0)

        def narrow(n, carry):
            du_buf[chunk_rows(n, q), :] = work[n, q * CHUNK : (q + 1) * CHUNK, :].astype(BF16)
            return carry

        lax.fori_loop(0, count, narrow, 0, unroll=8)
        du_got[chunk_rows(me, q), :] = du_buf[chunk_rows(me, q), :]
        each_peer(lambda p: send(du_buf.at[chunk_rows(p, q)], du_got.at[chunk_rows(me, q)], DU + q, {"ctx": p}))
        send_some(q + 1)

    def filter_grad(q, i, carry):
        rows = rows_of(i, STEP * count)
        spec = forward(gather_rows(u_got.at[q], (i - q * steps) * STEP, count), first_two, twist, second, True)
        scatter_rows(gf_buf, i * STEP, inverse(conj_product(spec_dy[rows, :], spec), twist, third, last))
        return carry

    def filter_chunk(q):
        wait_for(recv_sem, U + q, u_got.at[q, others])
        lax.fori_loop(q * steps, (q + 1) * steps, functools.partial(filter_grad, q), 0)

    unfilled = list(range(CHUNKS))

    def fill(position):
        for _ in range(FILLS[position]):
            filter_chunk(unfilled.pop(0))

    fill(0)

    for q in range(CHUNKS):
        wait_for(recv_sem, DU + q, dy_got.at[q, others])
    r_mine[...] = dot(b_ref[...], du_got[...])
    each_group(lambda g: send(r_mine, r_got.at[grp], 1, {"grp": g}))

    blocks = width // LANES
    half = ranks * blocks

    def outer(value, tokens, offset):
        first, rest = split(value)
        both = dot(jnp.concatenate([first, rest], axis=0), tokens, ((1,), (1,)))
        out = (both[:ranks] + both[ranks:]) * factor
        for k in range(blocks):
            parts[pl.ds(offset + k, ranks, stride=blocks), :] = out[:, k * LANES : (k + 1) * LANES]

    def tile_of(p):
        return rows_of(p % 2 * (count // 2) + p // 2, 8)

    def send_parts(role):
        each_owner(role, lambda p: send(parts.at[tile_of(p)], part_got.at[me], 2, {"ctx": p}))

    outer(z, du_got[...], half)
    send_parts(1)
    wait_for(recv_sem, 1, r_got.at[pl.ds(0, groups - 1)])
    rank_grad = shared_sum(r_mine, r_got)
    outer(rank_grad, x_buf[...], 0)
    send_parts(0)
    part_got[me] = parts[tile_of(me), :]
    low_rank(lambda s, n: du_got[s : s + n, :], a_ref, rank_grad, gi_ref)

    fill(1)
    wait_for(recv_sem, 2, part_got.at[others])
    acc = jnp.sum(part_got[...], axis=0)
    total[...] = acc
    total_got[tile_of(me), :] = acc
    each_peer(lambda p: send(total, total_got.at[tile_of(me)], 3, {"ctx": p}))
    fill(2)

    def store_gf(n, carry):
        pltpu.make_async_copy(gf_buf.at[n], gf_ref.at[:, lanes_of(n)], load_sem.at[11]).start()
        return carry

    lax.fori_loop(0, count, store_gf, 0)

    wait_for(recv_sem, 3, part_got.at[others])
    gd_ref[...] = total_got[pl.ds(0, half), :]
    gu_ref[...] = total_got[pl.ds(half, half), :]

    pltpu.make_async_copy(gf_buf, gf_buf, load_sem.at[11]).wait()
    for slot in range(2):
        wait_for(send_sem, slot, z_got.at[pl.ds(0, groups - 1)])
    for slot in range(2, 4):
        wait_for(send_sem, slot, part_got.at[others])
    for slot in range(DY, DY + 3 * CHUNKS):
        wait_for(send_sem, slot, dy_got.at[0, others])


def store_kernel(gi, gf, gd, gu, gi_out, gf_out, gd_out, gu_out, sems):
    copies = [
        pltpu.make_async_copy(src, dst, sems.at[k])
        for k, (src, dst) in enumerate([(gf, gf_out), (gi, gi_out), (gd, gd_out), (gu, gu_out)])
    ]
    for copy in copies:
        copy.start()
    for copy in copies:
        copy.wait()


def body(count, groups, saved_input, out_grad, filters, adapter_down, adapter_up):
    width, tokens = saved_input.shape[1], filters.shape[2]
    ranks = adapter_down.shape[0]
    tables = [jnp.asarray(t) for t in make_tables(count)]
    rows = count * CHANS
    hbm = pl.BlockSpec(memory_space=pl.ANY)
    source = pl.BlockSpec(memory_space=SOURCE)
    spec = pltpu.VMEM((rows, 2 * LANES), F32)
    small = pltpu.VMEM((ranks, LANES), F32)
    some = pltpu.VMEM((groups, ranks, LANES), F32)
    narrow = pltpu.VMEM((rows, LANES), BF16)
    wide = pltpu.VMEM((count, CHANS, LANES), F32)
    maps = pltpu.VMEM((ranks, width), BF16)
    tiles = pltpu.VMEM((count * 8, LANES), F32)
    got = pltpu.VMEM((CHUNKS, count, CHUNK, LANES), BF16)
    flat = ranks * width // LANES
    results = pl.pallas_call(
        functools.partial(kernel, count, groups, float(tokens) ** -0.5),
        out_shape=(
            pltpu.VMEM((width, LANES), BF16),
            pltpu.VMEM((CHANS, tokens), F32),
            pltpu.VMEM((flat, LANES), F32),
            pltpu.VMEM((flat, LANES), F32),
        ),
        in_specs=[source] * 11,
        out_specs=(pl.BlockSpec(memory_space=pltpu.VMEM),) * 4,
        scratch_shapes=[
            maps, maps, *[pltpu.VMEM(t.shape, t.dtype) for t in tables],
            narrow, wide, narrow, narrow, got, got, narrow, wide, wide,
            spec, spec, small, some, small, some, tiles, pltpu.VMEM((count, 8, LANES), F32),
            pltpu.VMEM((8, LANES), F32), tiles,
            pltpu.SemaphoreType.DMA((12 + CHUNKS,)),
            pltpu.SemaphoreType.DMA((4 + 3 * CHUNKS,)),
            pltpu.SemaphoreType.DMA((4 + 3 * CHUNKS,)),
        ],
        compiler_params=pltpu.CompilerParams(
            collective_id=0, has_side_effects=True, vmem_limit_bytes=VMEM_LIMIT
        ),
    )(saved_input[0], out_grad[0], filters[0], adapter_down[:, 0, :], adapter_up[:, 0, :], *tables)
    grad_input, grad_filter, down, up = pl.pallas_call(
        store_kernel,
        out_shape=tuple(jax.ShapeDtypeStruct(r.shape, r.dtype) for r in results),
        in_specs=[pl.BlockSpec(memory_space=pltpu.VMEM)] * 4,
        out_specs=(hbm,) * 4,
        scratch_shapes=[pltpu.SemaphoreType.DMA((4,))],
    )(*[pltpu.with_memory_space_constraint(r, pltpu.VMEM) for r in results])
    return (
        grad_input[None],
        grad_filter[None],
        down.reshape(ranks, 1, width),
        up.reshape(ranks, 1, width),
    )


def solution(mesh):
    placed = (
        P("grp", None, "ctx"),
        P("grp", None, "ctx"),
        P("grp", "ctx", None),
        P(None, "grp", None),
        P(None, "grp", None),
    )
    return jax.shard_map(
        functools.partial(body, mesh.shape["ctx"], mesh.shape["grp"]),
        mesh=mesh,
        in_specs=placed,
        out_specs=(
            P("grp", None, "ctx"),
            P("grp", "ctx", None),
            P(None, "grp", None),
            P(None, "grp", None),
        ),
        check_vma=False,
    )
```

```python
import functools
import math

import jax
import jax.numpy as jnp
import numpy as np
from jax import lax
from jax.experimental import pallas as pl
from jax.experimental.pallas import tpu as pltpu
from jax.sharding import PartitionSpec as P

MESH = pl.DeviceIdType.MESH
F32 = jnp.float32
BF16 = jnp.bfloat16
LANES = 128
CHANS = 32
STEP = 16
CHUNK = 16
CHUNKS = CHANS // CHUNK
SENDS = (1, 0, 1)
FILLS = (1, 1, 0)
GROUP_ORDER = (1, 2, 3)
FAR = True
DY, U, DU = 4, 4 + CHUNKS, 4 + 2 * CHUNKS
GRID = {64: (4, 4, 2, 2), 8: (2, 2, 1, 2)}
VMEM_LIMIT = 56 * 1024 * 1024
SOURCE = pl.ANY


def far_first(high, wide, direct):
    def hops(i):
        down, across = i // wide, i % wide
        return min(down, high - down) + min(across, wide - across)

    order = sorted(range(1, high * wide), key=lambda i: (-hops(i), i) if direct else i)
    late = [k for k, i in enumerate(order[:8]) if i < 8]
    if len(order) > 8:
        order.insert(7, order.pop(late[-1]))
    codes = [sum(i << (4 * k) for k, i in enumerate(part)) for part in (order[:8], order[8:])]
    return len(order), codes


def halves(table):
    high = table.astype(BF16)
    low = (table - high.astype(np.float64)).astype(BF16)
    return high, low


def make_tables(rows):
    points = 2 * rows * LANES
    n = np.arange(rows)
    p = np.arange(LANES)
    theta = np.outer(n + 0.5, n) * (2.0 * math.pi / (2 * rows))
    phi = np.outer(p, p) * (2.0 * math.pi / LANES)
    turn = np.outer(n + 0.5, p) * (2.0 * math.pi / points)
    high, low = halves(np.concatenate([np.cos(theta), -np.sin(theta)], axis=0))
    first_two = np.concatenate([high, low], axis=1)
    first_three = np.concatenate([high, high, low], axis=1)
    cos, sin = np.cos(phi), np.sin(phi)
    high, low = halves(np.block([[cos, -sin], [sin, cos]]))
    second = np.concatenate([high, high, low], axis=0)
    high, low = halves(np.block([[cos, sin], [-sin, cos]]))
    third = np.concatenate([high, high, low], axis=0)
    high, low = halves(np.concatenate([np.cos(theta).T, -np.sin(theta).T], axis=1) * (2.0 / points))
    last = np.concatenate([high, high, low], axis=1)
    twist = np.stack([np.cos(turn), np.sin(turn)]).astype(np.float32)
    return first_two, first_three, twist, second, third, last


def split(value):
    high = value.astype(BF16)
    return high, (value - high.astype(F32)).astype(BF16)


def dot(left, right, dims=((1,), (0,))):
    return lax.dot_general(left, right, (dims, ((), ())), preferred_element_type=F32)


def gather_rows(ref, first, rows):
    block = ref[:, pl.ds(pl.multiple_of(first, STEP), STEP), :].astype(F32)
    turned = jnp.swapaxes(block, 0, 1)
    return jnp.concatenate([turned[j] for j in range(STEP)], axis=1)


def forward(data, first, twist, second, exact):
    rows = data.shape[0]
    if exact:
        narrow = data.astype(BF16)
        stacked = jnp.concatenate([narrow, narrow], axis=0)
    else:
        high, low = split(data)
        stacked = jnp.concatenate([high, low, high], axis=0)
    part = dot(first[...], stacked)
    cos, sin = twist[0], twist[1]
    joined = []
    for j in range(STEP):
        lanes = slice(j * LANES, (j + 1) * LANES)
        real, imag = part[:rows, lanes], part[rows:, lanes]
        joined.append(jnp.concatenate([real * cos + imag * sin, imag * cos - real * sin], axis=1))
    high, low = split(jnp.concatenate(joined, axis=0))
    return dot(jnp.concatenate([high, low, high], axis=1), second[...])


def inverse(spectrum, twist, third, last):
    rows = twist.shape[1]
    high, low = split(spectrum)
    part = dot(jnp.concatenate([high, low, high], axis=1), third[...])
    cos, sin = twist[0], twist[1]
    reals, imags = [], []
    for j in range(STEP):
        real = part[j * rows : (j + 1) * rows, :LANES]
        imag = part[j * rows : (j + 1) * rows, LANES:]
        reals.append(real * cos - imag * sin)
        imags.append(real * sin + imag * cos)
    joined = jnp.concatenate([jnp.concatenate(reals, axis=1), jnp.concatenate(imags, axis=1)], axis=0)
    high, low = split(joined)
    return dot(last[...], jnp.concatenate([high, low, high], axis=0))


def conj_product(left, right):
    lr, li = left[:, :LANES], left[:, LANES:]
    rr, ri = right[:, :LANES], right[:, LANES:]
    return jnp.concatenate([lr * rr + li * ri, li * rr - lr * ri], axis=1)


def kernel(
    count, groups, factor,
    x_hbm, dy_hbm, h_hbm, a_hbm, b_hbm, first_two_hbm, first_three_hbm, twist_hbm, second_hbm, third_hbm, last_hbm,
    gi_ref, gf_ref, gd_ref, gu_ref,
    a_ref, b_ref, first_two, first_three, twist, second, third, last,
    x_buf, h_buf, u_buf, du_buf, dy_got, u_got, du_got, work, gf_buf,
    spec_h, spec_dy, z_mine, z_got, r_mine, r_got, parts, part_got, total, total_got,
    load_sem, send_sem, recv_sem,
):
    me = lax.axis_index("ctx")
    grp = lax.axis_index("grp")
    high, wide_x, deep, cores = GRID[count]
    core, near = me % cores, me % (deep * cores) // cores
    place = me // (deep * cores)
    down, across = place // wide_x, place % wide_x
    chips, codes = far_first(high, wide_x, FAR)
    width = count * CHANS
    ranks = a_ref.shape[0]
    inner = [
        ((near + k // cores) % deep) * cores + (core + k % cores) % cores
        for k in reversed(range(deep * cores))
    ]
    sides = [((near + k) % deep) * cores for k in reversed(range(deep))]

    def chip(t):
        code = jnp.where(t < 8, codes[0], codes[1])
        i = (code >> (4 * (t & 7))) & 15
        row = (down + i // wide_x if wide_x != 4 else down + (i >> 2)) & (high - 1)
        column = (across + i) & (wide_x - 1)
        return (row * wide_x + column) * (deep * cores)

    def each_peer(action):
        def run(t, carry):
            base = chip(t)
            for offset in inner:
                action(base + offset)
            return carry

        lax.fori_loop(0, chips, run, 0)
        for offset in inner[:-1]:
            action(place * deep * cores + offset)

    def each_owner(role, action):
        def run(t, carry):
            base = chip(t)
            for side in sides:
                action(base + side + role)
            return carry

        lax.fori_loop(0, chips, run, 0)
        for side in sides[:-1]:
            action(place * deep * cores + side + role)

        @pl.when(core != role)
        def _():
            action(place * deep * cores + sides[-1] + role)

    def each_group(action):
        for e in GROUP_ORDER:
            if e < groups:
                action(lax.rem(grp + e, groups))

    def send(src, dst, slot, target):
        pltpu.make_async_remote_copy(
            src_ref=src, dst_ref=dst, send_sem=send_sem.at[slot], recv_sem=recv_sem.at[slot],
            device_id=target, device_id_type=MESH,
        ).start()

    def wait_for(sems, slot, ref):
        pltpu.make_async_copy(ref, ref, sems.at[slot]).wait()

    def rows_of(n, size):
        return pl.ds(pl.multiple_of(n * size, size), size)

    def lanes_of(n):
        return pl.ds(pl.multiple_of(n * LANES, LANES), LANES)

    def chunk_rows(p, q):
        return pl.ds(pl.multiple_of(p * CHANS + q * CHUNK, CHUNK), CHUNK)

    barrier = pltpu.get_barrier_semaphore()

    def greet(target):
        pl.semaphore_signal(barrier, inc=1, device_id=target, device_id_type=MESH)

    each_peer(lambda p: greet({"ctx": p}))
    each_group(lambda g: greet({"grp": g}))

    loads = [
        pltpu.make_async_copy(src, dst, load_sem.at[k])
        for k, (src, dst) in enumerate(
            [
                (a_hbm, a_ref), (x_hbm, x_buf), (first_three_hbm, first_three), (twist_hbm, twist),
                (second_hbm, second), (b_hbm, b_ref), (first_two_hbm, first_two), (third_hbm, third),
                (last_hbm, last),
            ]
        )
    ]
    for load in loads:
        load.start()

    def load_h(n, carry):
        pltpu.make_async_copy(h_hbm.at[:, lanes_of(n)], h_buf.at[n], load_sem.at[9]).start()
        return carry

    lax.fori_loop(0, count, load_h, 0)
    own = [
        pltpu.make_async_copy(dy_hbm.at[chunk_rows(me, q)], dy_got.at[q, me], load_sem.at[12 + q])
        for q in range(CHUNKS)
    ]
    for copy in own:
        copy.start()
    loads[0].wait()
    loads[1].wait()
    z_mine[...] = dot(a_ref[...], x_buf[...])
    pl.semaphore_wait(barrier, count - 1 + groups - 1)

    each_group(lambda g: send(z_mine, z_got.at[grp], 0, {"grp": g}))
    for q in range(CHUNKS):
        each_peer(lambda p: send(dy_hbm.at[chunk_rows(p, q)], dy_got.at[q, me], DY + q, {"ctx": p}))

    pltpu.make_async_copy(h_buf, h_buf, load_sem.at[9]).wait()
    for load in loads[2:]:
        load.wait()

    def spectrum_h(i, carry):
        data = gather_rows(h_buf, i * STEP, count)
        spec_h[rows_of(i, STEP * count), :] = forward(data, first_three, twist, second, False)
        return carry

    lax.fori_loop(0, CHANS // STEP, spectrum_h, 0)

    def shared_sum(mine, got):
        got[grp] = mine[...]
        acc = got[0]
        for g in range(1, groups):
            acc = acc + got[g]
        return acc

    def low_rank(base, maps, value, out):
        high_part, low_part = split(value)
        pair = jnp.concatenate([high_part, low_part], axis=0)
        chunk = 256
        for start in range(0, width, chunk):
            left = maps[:, start : start + chunk]
            left = jnp.concatenate([left, left], axis=0)
            extra = dot(left, pair, ((0,), (0,)))
            out[start : start + chunk, :] = (base(start, chunk).astype(F32) + extra).astype(BF16)

    wait_for(recv_sem, 0, z_got.at[pl.ds(0, groups - 1)])
    z = shared_sum(z_mine, z_got)
    low_rank(lambda s, n: x_buf[s : s + n, :], b_ref, z, u_buf)
    for q in range(CHUNKS):
        u_got[q, me] = u_buf[chunk_rows(me, q), :]

    def send_u(q):
        each_peer(lambda p: send(u_buf.at[chunk_rows(p, q)], u_got.at[q, me], U + q, {"ctx": p}))

    pending = list(range(CHUNKS))

    def send_some(position):
        for _ in range(SENDS[position]):
            send_u(pending.pop(0))

    send_some(0)

    others = pl.ds(0, count - 1)

    def scatter_rows(ref, first, value):
        turned = jnp.stack([value[:, j * LANES : (j + 1) * LANES] for j in range(STEP)])
        ref[:, pl.ds(pl.multiple_of(first, STEP), STEP), :] = jnp.swapaxes(turned, 0, 1)

    def conv_grad(q, i, carry):
        rows = rows_of(i, STEP * count)
        spec = forward(gather_rows(dy_got.at[q], (i - q * steps) * STEP, count), first_two, twist, second, True)
        spec_dy[rows, :] = spec
        scatter_rows(work, i * STEP, inverse(conj_product(spec, spec_h[rows, :]), twist, third, last))
        return carry

    steps = CHUNK // STEP
    for q in range(CHUNKS):
        own[q].wait()
        wait_for(recv_sem, DY + q, dy_got.at[q, others])
        lax.fori_loop(q * steps, (q + 1) * steps, functools.partial(conv_grad, q), 0)

        def narrow(n, carry):
            du_buf[chunk_rows(n, q), :] = work[n, q * CHUNK : (q + 1) * CHUNK, :].astype(BF16)
            return carry

        lax.fori_loop(0, count, narrow, 0, unroll=8)
        du_got[chunk_rows(me, q), :] = du_buf[chunk_rows(me, q), :]
        each_peer(lambda p: send(du_buf.at[chunk_rows(p, q)], du_got.at[chunk_rows(me, q)], DU + q, {"ctx": p}))
        send_some(q + 1)

    def filter_grad(q, i, carry):
        rows = rows_of(i, STEP * count)
        spec = forward(gather_rows(u_got.at[q], (i - q * steps) * STEP, count), first_two, twist, second, True)
        scatter_rows(gf_buf, i * STEP, inverse(conj_product(spec_dy[rows, :], spec), twist, third, last))
        return carry

    def filter_chunk(q):
        wait_for(recv_sem, U + q, u_got.at[q, others])
        lax.fori_loop(q * steps, (q + 1) * steps, functools.partial(filter_grad, q), 0)

    unfilled = list(range(CHUNKS))

    def fill(position):
        for _ in range(FILLS[position]):
            filter_chunk(unfilled.pop(0))

    fill(0)

    for q in range(CHUNKS):
        wait_for(recv_sem, DU + q, dy_got.at[q, others])
    r_mine[...] = dot(b_ref[...], du_got[...])
    each_group(lambda g: send(r_mine, r_got.at[grp], 1, {"grp": g}))

    blocks = width // LANES
    half = ranks * blocks

    def outer(value, tokens, offset):
        first, rest = split(value)
        both = dot(jnp.concatenate([first, rest], axis=0), tokens, ((1,), (1,)))
        out = (both[:ranks] + both[ranks:]) * factor
        for k in range(blocks):
            parts[pl.ds(offset + k, ranks, stride=blocks), :] = out[:, k * LANES : (k + 1) * LANES]

    def tile_of(p):
        return rows_of(p % 2 * (count // 2) + p // 2, 8)

    def send_parts(role):
        each_owner(role, lambda p: send(parts.at[tile_of(p)], part_got.at[me], 2, {"ctx": p}))

    outer(z, du_got[...], half)
    send_parts(1)
    wait_for(recv_sem, 1, r_got.at[pl.ds(0, groups - 1)])
    rank_grad = shared_sum(r_mine, r_got)
    outer(rank_grad, x_buf[...], 0)
    send_parts(0)
    part_got[me] = parts[tile_of(me), :]

    fill(1)
    wait_for(recv_sem, 2, part_got.at[others])
    acc = jnp.sum(part_got[...], axis=0)
    total[...] = acc
    total_got[tile_of(me), :] = acc
    each_peer(lambda p: send(total, total_got.at[tile_of(me)], 3, {"ctx": p}))
    low_rank(lambda s, n: du_got[s : s + n, :], a_ref, rank_grad, gi_ref)
    fill(2)

    def store_gf(n, carry):
        pltpu.make_async_copy(gf_buf.at[n], gf_ref.at[:, lanes_of(n)], load_sem.at[11]).start()
        return carry

    lax.fori_loop(0, count, store_gf, 0)

    wait_for(recv_sem, 3, part_got.at[others])
    gd_ref[...] = total_got[pl.ds(0, half), :]
    gu_ref[...] = total_got[pl.ds(half, half), :]

    pltpu.make_async_copy(gf_buf, gf_buf, load_sem.at[11]).wait()
    for slot in range(2):
        wait_for(send_sem, slot, z_got.at[pl.ds(0, groups - 1)])
    for slot in range(2, 4):
        wait_for(send_sem, slot, part_got.at[others])
    for slot in range(DY, DY + 3 * CHUNKS):
        wait_for(send_sem, slot, dy_got.at[0, others])


def store_kernel(gi, gf, gd, gu, gi_out, gf_out, gd_out, gu_out, sems):
    copies = [
        pltpu.make_async_copy(src, dst, sems.at[k])
        for k, (src, dst) in enumerate([(gf, gf_out), (gi, gi_out), (gd, gd_out), (gu, gu_out)])
    ]
    for copy in copies:
        copy.start()
    for copy in copies:
        copy.wait()


def body(count, groups, saved_input, out_grad, filters, adapter_down, adapter_up):
    width, tokens = saved_input.shape[1], filters.shape[2]
    ranks = adapter_down.shape[0]
    tables = [jnp.asarray(t) for t in make_tables(count)]
    rows = count * CHANS
    hbm = pl.BlockSpec(memory_space=pl.ANY)
    source = pl.BlockSpec(memory_space=SOURCE)
    spec = pltpu.VMEM((rows, 2 * LANES), F32)
    small = pltpu.VMEM((ranks, LANES), F32)
    some = pltpu.VMEM((groups, ranks, LANES), F32)
    narrow = pltpu.VMEM((rows, LANES), BF16)
    wide = pltpu.VMEM((count, CHANS, LANES), F32)
    maps = pltpu.VMEM((ranks, width), BF16)
    tiles = pltpu.VMEM((count * 8, LANES), F32)
    got = pltpu.VMEM((CHUNKS, count, CHUNK, LANES), BF16)
    flat = ranks * width // LANES
    results = pl.pallas_call(
        functools.partial(kernel, count, groups, float(tokens) ** -0.5),
        out_shape=(
            pltpu.VMEM((width, LANES), BF16),
            pltpu.VMEM((CHANS, tokens), F32),
            pltpu.VMEM((flat, LANES), F32),
            pltpu.VMEM((flat, LANES), F32),
        ),
        in_specs=[source] * 11,
        out_specs=(pl.BlockSpec(memory_space=pltpu.VMEM),) * 4,
        scratch_shapes=[
            maps, maps, *[pltpu.VMEM(t.shape, t.dtype) for t in tables],
            narrow, wide, narrow, narrow, got, got, narrow, wide, wide,
            spec, spec, small, some, small, some, tiles, pltpu.VMEM((count, 8, LANES), F32),
            pltpu.VMEM((8, LANES), F32), tiles,
            pltpu.SemaphoreType.DMA((12 + CHUNKS,)),
            pltpu.SemaphoreType.DMA((4 + 3 * CHUNKS,)),
            pltpu.SemaphoreType.DMA((4 + 3 * CHUNKS,)),
        ],
        compiler_params=pltpu.CompilerParams(
            collective_id=0, has_side_effects=True, vmem_limit_bytes=VMEM_LIMIT
        ),
    )(saved_input[0], out_grad[0], filters[0], adapter_down[:, 0, :], adapter_up[:, 0, :], *tables)
    grad_input, grad_filter, down, up = pl.pallas_call(
        store_kernel,
        out_shape=tuple(jax.ShapeDtypeStruct(r.shape, r.dtype) for r in results),
        in_specs=[pl.BlockSpec(memory_space=pltpu.VMEM)] * 4,
        out_specs=(hbm,) * 4,
        scratch_shapes=[pltpu.SemaphoreType.DMA((4,))],
    )(*[pltpu.with_memory_space_constraint(r, pltpu.VMEM) for r in results])
    return (
        grad_input[None],
        grad_filter[None],
        down.reshape(ranks, 1, width),
        up.reshape(ranks, 1, width),
    )


def solution(mesh):
    placed = (
        P("grp", None, "ctx"),
        P("grp", None, "ctx"),
        P("grp", "ctx", None),
        P(None, "grp", None),
        P(None, "grp", None),
    )
    return jax.shard_map(
        functools.partial(body, mesh.shape["ctx"], mesh.shape["grp"]),
        mesh=mesh,
        in_specs=placed,
        out_specs=(
            P("grp", None, "ctx"),
            P("grp", "ctx", None),
            P(None, "grp", None),
            P(None, "grp", None),
        ),
        check_vma=False,
    )
```
